32 devices in a mesh: gx: 4 (over z), gy: 4 (over y, core), gz: 2 (over x).
Axes of the slice: x: 2, y: 2, z: 4, core: 2. Of those that a mesh axis runs over, the one named last changes fastest.
Arguments:
- features: bfloat16 [64, 8, 32, 256], P(None, 'gx', 'gy', 'gz'), may hold values from -6 to 6
- dest_bricks: int32 [1024, 1], P(('gx', 'gy', 'gz')), may hold values from 0 to 7
- cell_ids: int32 [1024, 64], P(('gx', 'gy', 'gz')), may hold values from 0 to 2047
- cic_masses: bfloat16 [1024, 64], P(('gx', 'gy', 'gz')), may hold values from 0.25 to 4
- live_counts: int32 [32], P(('gx', 'gy', 'gz')), may hold values from 8 to 32
- style_vector: float32 [512], replicated, may hold values from -6 to 6
- affine_first: float32 [512, 64], replicated, may hold values from -0.25 to 0.25
- kernel_first: bfloat16 [27, 64, 64], replicated, may hold values from -0.15625 to 0.15625
- bias_first: float32 [64], replicated, may hold values from -0.5 to 0.5
- gain_first: float32 [64], replicated, may hold values from 1 to 4
- affine_second: float32 [512, 64], replicated, may hold values from -0.25 to 0.25
- kernel_second: bfloat16 [27, 64, 64], replicated, may hold values from -0.15625 to 0.15625
- bias_second: float32 [64], replicated, may hold values from -0.5 to 0.5
- gain_second: float32 [64], replicated, may hold values from 1 to 4
Outputs:
- upsampled: bfloat16 [64, 8, 32, 256], P(None, 'gx', 'gy', 'gz')
The draws below stay inside these ranges and needn't reach their ends.
All inputs are finite; a program needn't handle non-finite values.
Results may differ from the reference program's by a relative error of at most 0.0054.
Values may be sent and summed in bfloat16 or wider, within the bound.
No kernel may reach another device: no remote copies, remote signals or barrier semaphores. Data moves between devices by JAX's collectives and lax.ppermute only.
A program may use at most 64 MiB of HBM per device.

```python
import math
import jax
import jax.numpy as jnp
from jax import lax

C = 64
STYLE = 512
BX = 2
BY = 8
BZ = 128
NB = 32
PB = 64
CELLS = 2048
GROUP = 8
BLOCKS = 1024
NX = 8
NY = 32
NZ = 256
N_GX = 4
N_GY = 4
N_GZ = 2
DEVICES = 32


def with_ends(entries, key, least, high):
    longest = entries.shape.index(max(entries.shape))
    spots = []
    for shift in (0, 1):
        where = [jax.random.randint(jax.random.fold_in(key, axis), (), 0, length) for axis, length in enumerate(entries.shape)]
        where[longest] = (where[longest] + shift) % entries.shape[longest]
        spots.append(tuple(where))
    return entries.at[spots[0]].set(least).at[spots[1]].set(high)


def level_of(own_key, shape, split, smallest, high):
    level = 1.0
    for axis_at, parts in split:
        steps = jax.random.uniform(jax.random.fold_in(jax.random.fold_in(own_key, 6), axis_at), (parts,), jnp.float32, smallest / len(split), high / len(split))
        level = level * jnp.repeat(jnp.exp(steps), shape[axis_at] // parts).reshape((-1,) + (1,) * (len(shape) - 1 - axis_at))
    return level


def different_ones(rng, rows, amount, top, lift):
    order = jax.random.permutation(jax.random.fold_in(rng, 1), amount)
    boost = order
    for power in range(3):
        boost = boost * boost // amount
    boost = boost * lift // amount
    lots = jax.random.randint(jax.random.fold_in(rng, 2), (rows, amount), 0, 4096) + boost
    holders = jax.random.permutation(jax.random.fold_in(rng, 3), rows)[jnp.arange(amount) % rows]
    lots = jnp.where(jnp.arange(rows)[:, None] == holders[None, :], 1 << 14, lots)
    priority = lots * amount + jnp.arange(amount)
    return lax.top_k(priority.astype(jnp.int32), top)[1].astype(jnp.int32)


def centred(rng, shape, spread, reach, split=(), held_as=jnp.bfloat16):
    values = jax.random.normal(rng, shape, jnp.float32) * spread
    if len(split) > 0:
        values = level_of(rng, shape, split, -0.22, 0.18) * values
    return jnp.clip(values, min=-reach, max=reach).astype(held_as)


def setup_inputs(seed: int = 0) -> dict:
    key_of = jax.random.split(jax.random.key(seed), 15)
    features = centred(key_of[0], (C, NX, NY, NZ), 1.0, 6.0, ((1, 4), (2, 4), (3, 2)))
    dest_bricks = different_ones(key_of[1], BLOCKS, GROUP, 1, 2048)
    cell_ids = with_ends(jax.random.randint(key_of[2], (BLOCKS, PB), 0, CELLS), jax.random.fold_in(key_of[2], 1), 0, CELLS - 1).astype(jnp.int32)
    cic_masses = jnp.clip(0.25 + 3.75 * jax.random.uniform(key_of[3], (BLOCKS, PB), jnp.float32) ** level_of(key_of[3], (BLOCKS, PB), ((0, 32),), -0.2, 0.2), 0.25, 4.0).astype(jnp.bfloat16)
    live_counts = with_ends(jax.random.randint(key_of[4], (DEVICES,), NB // 4, NB + 1), jax.random.fold_in(key_of[4], 1), NB // 4, NB).astype(jnp.int32)
    style_vector = centred(key_of[5], (STYLE,), 1.0, 6.0, (), jnp.float32)
    affine_first = centred(key_of[6], (STYLE, C), STYLE ** -0.5, 0.25, (), jnp.float32)
    kernel_first = centred(key_of[7], (27, C, C), (27 * C) ** -0.5, 0.15625)
    bias_first = jnp.clip(jax.random.uniform(key_of[8], (C,), jnp.float32, -0.5, 0.5), -0.5, 0.5)
    gain_first = jnp.clip(jnp.exp(jax.random.uniform(key_of[9], (C,), jnp.float32, math.log(1.0), math.log(4.0))), 1.0, 4.0)
    affine_second = centred(key_of[10], (STYLE, C), STYLE ** -0.5, 0.25, (), jnp.float32)
    kernel_second = centred(key_of[11], (27, C, C), (27 * C) ** -0.5, 0.15625)
    bias_second = jnp.clip(jax.random.uniform(key_of[12], (C,), jnp.float32, -0.5, 0.5), -0.5, 0.5)
    gain_second = jnp.clip(jnp.exp(jax.random.uniform(key_of[13], (C,), jnp.float32, math.log(1.0), math.log(4.0))), 1.0, 4.0)
    return dict(features=features, dest_bricks=dest_bricks, cell_ids=cell_ids, cic_masses=cic_masses, live_counts=live_counts, style_vector=style_vector, affine_first=affine_first, kernel_first=kernel_first, bias_first=bias_first, gain_first=gain_first, affine_second=affine_second, kernel_second=kernel_second, bias_second=bias_second, gain_second=gain_second)


def modulate(kernel, style_vector, affine):
    styles = jnp.dot(style_vector[None, :], affine, precision=lax.Precision.HIGHEST, preferred_element_type=jnp.float32)[0] + 1.0
    scaled = kernel.astype(jnp.float32) * styles[None, None, :]
    demod = lax.rsqrt(lax.optimization_barrier(jnp.sum(scaled * scaled, axis=(0, 2))) + 1e-08)
    return (scaled * demod[None, :, None]).astype(jnp.bfloat16)

def activate(values):
    return jnp.where(values >= 0, values, 0.2 * values) * jnp.sqrt(jnp.float32(2.0))

def styled_layer(inputs, kernel, style_vector, affine, bias, gain, density):
    modulated = modulate(kernel, style_vector, affine).astype(jnp.float32)
    chans = modulated.shape[1]
    kernel_full = modulated.reshape(3, 3, 3, chans, chans).transpose(3, 4, 0, 1, 2)
    padded = jnp.pad(inputs.astype(jnp.float32), ((0, 0), (1, 1), (1, 1), (1, 1)), mode='wrap')
    convolved = lax.conv_general_dilated(padded[None], kernel_full, (1, 1, 1), 'VALID', dimension_numbers=('NCDHW', 'OIDHW', 'NCDHW'), precision=lax.Precision.HIGHEST)[0]
    summed = convolved + gain[:, None, None, None] * density[None] + bias[:, None, None, None]
    return activate(summed)

def reference(features, dest_bricks, cell_ids, cic_masses, live_counts, style_vector, affine_first, kernel_first, bias_first, gain_first, affine_second, kernel_second, bias_second, gain_second):
    block_index = jnp.arange(BLOCKS, dtype=jnp.int32)
    source = block_index // NB
    live = block_index % NB < live_counts[source]
    slab = source // GROUP
    brick = slab * GROUP + dest_bricks[:, 0]
    flat = (brick[:, None] * CELLS + cell_ids).reshape(-1).astype(jnp.int32)
    masses = (cic_masses.astype(jnp.float32) * live[:, None].astype(jnp.float32)).reshape(-1)
    painted = jax.ops.segment_sum(masses, flat, num_segments=DEVICES * CELLS)
    density = painted.reshape(N_GX, N_GY, N_GZ, BX, BY, BZ).transpose(0, 3, 1, 4, 2, 5).reshape(NX, NY, NZ)
    hidden = styled_layer(features, kernel_first, style_vector, affine_first, bias_first, gain_first, density).astype(jnp.bfloat16)
    result = styled_layer(hidden, kernel_second, style_vector, affine_second, bias_second, gain_second, density)
    return result.astype(jnp.bfloat16)
```

```python
import functools

import jax
import jax.numpy as jnp
from jax import lax
from jax.experimental import pallas as pl
from jax.experimental.pallas import tpu as pltpu
from jax.sharding import PartitionSpec as P

F32 = jnp.float32
BF16 = jnp.bfloat16
SMEM = pltpu.SMEM


def shift(cells, axis, step):
    count = lax.axis_size(axis)
    return lax.ppermute(cells, axis, [(i, (i + step) % count) for i in range(count)])


def call(body, outs, name, flops=0, smem=(), scratch=()):
    def run(*args):
        size = sum(a.size * a.dtype.itemsize for a in args)
        specs = [
            pl.BlockSpec(memory_space=SMEM if i in smem else pltpu.VMEM)
            for i in range(len(args))
        ]
        return pl.pallas_call(
            body,
            out_shape=tuple(jax.ShapeDtypeStruct(s, d) for s, d in outs),
            in_specs=specs,
            out_specs=tuple(pl.BlockSpec(memory_space=pltpu.VMEM) for _ in outs),
            scratch_shapes=list(scratch),
            name=name,
            cost_estimate=pl.CostEstimate(
                flops=flops, bytes_accessed=size, transcendentals=0
            ),
        )(*args)

    return run


def lanes_of(shape):
    return lax.broadcasted_iota(jnp.int32, shape, len(shape) - 1)


def rolled(values, amount, axis):
    amount = amount % values.shape[axis]
    return values if amount == 0 else pltpu.roll(values, amount, axis)


def halves(values):
    high = values.astype(BF16)
    return high, (values - high.astype(F32)).astype(BF16)


def split_body(cells, *planes):
    for at, plane in enumerate(planes):
        part = cells[:, at].astype(F32)
        plane[...] = jnp.swapaxes(part, 0, 1).astype(BF16)


def column_of(row):
    size = row.shape[1]
    wide = jnp.broadcast_to(row, (size, size))
    same = lax.broadcasted_iota(jnp.int32, (size, size), 0) == lanes_of((size, size))
    return jnp.sum(jnp.where(same, wide, 0.0), axis=1, keepdims=True)


def modulate_body(style, affine, kernel, bias, gain, weights, columns):
    styles = (
        jnp.dot(
            style[...],
            affine[...],
            precision=lax.Precision.HIGHEST,
            preferred_element_type=F32,
        )
        + 1.0
    )
    chans = kernel.shape[1]
    total = jnp.zeros((chans, kernel.shape[2]), F32)
    for k in range(27):
        scaled = kernel[k].astype(F32) * styles
        total = total + scaled * scaled
    demod = lax.rsqrt(jnp.sum(total, axis=1, keepdims=True) + 1e-08)
    for g in range(3):
        blocks = [
            (kernel[3 * j + g].astype(F32) * styles * demod).astype(BF16)
            for j in range(9)
        ]
        weights[g * chans : (g + 1) * chans, :] = jnp.concatenate(blocks, axis=1)
    columns[0] = jnp.broadcast_to(column_of(bias[...]), columns.shape[1:])
    columns[1] = jnp.broadcast_to(column_of(gain[...]), columns.shape[1:])


def paint_body(rows_y, counts, where, live, dest, cells, masses, *refs):
    count_y, count_z = counts
    size_x = len(rows_y)
    planes, messages, own = refs[:size_x], refs[size_x:-1], refs[-1]
    size_y, chans, size_z = planes[0].shape
    blocks, per = cells.shape
    half = blocks // 2
    rank_y, rank_z = where[0], where[1]
    shape = (blocks, per)
    target = jnp.broadcast_to(dest[...], shape)
    to_y = lax.div(target, jnp.full(shape, count_z, jnp.int32))
    to_z = target - to_y * count_z - rank_z
    to_y = to_y - rank_y
    to_y = jnp.where(to_y < 0, to_y + count_y, to_y)
    to_z = jnp.where(to_z < 0, to_z + count_z, to_z)
    cell = cells[...]
    cell_row = lax.div(cell, jnp.full(shape, size_z, jnp.int32))
    at_z = cell - cell_row * size_z
    at_x = lax.div(cell_row, jnp.full(shape, size_y, jnp.int32))
    at_y = cell_row - at_x * size_y
    row = ((to_z * size_x + at_x) * count_y + to_y) * size_y + at_y
    alive = lax.broadcasted_iota(jnp.int32, shape, 0) < live[0]
    mass = jnp.where(alive, masses[...].astype(F32), 0.0)

    def paired(values):
        return jnp.concatenate([values[:half], values[half:]], axis=1)

    row, at_z, mass = paired(row), paired(at_z), paired(mass)
    width = 2 * per
    group = size_x * count_y * size_y
    total = count_z * group
    iota_rows = lax.broadcasted_iota(jnp.int32, (total, width), 0)
    iota_z = lax.broadcasted_iota(jnp.int32, (size_z, width), 0)
    left, right = [], []
    for r in range(half):
        left.append(
            jnp.where(iota_rows == row[r : r + 1], mass[r : r + 1], 0.0).astype(BF16)
        )
        right.append(jnp.where(iota_z == at_z[r : r + 1], 1.0, 0.0).astype(BF16))
    painted = lax.dot_general(
        jnp.concatenate(left, axis=1),
        jnp.concatenate(right, axis=1),
        (((1,), (1,)), ((), ())),
        preferred_element_type=F32,
    )
    parts = [painted[s * group : (s + 1) * group] for s in range(count_z)]
    lane = lanes_of((group, size_z))

    def beside(s):
        after = parts[(s + 1) % count_z]
        before = parts[(s - 1) % count_z]
        return jnp.where(lane == 0, after, jnp.where(lane == size_z - 1, before, 0.0))

    own[:group] = parts[0]
    own[group:] = beside(0)
    lane = lanes_of((chans, size_z))
    tile = jnp.zeros((chans, size_z), F32)
    for x in range(size_x):
        for y in range(size_y):
            j = x * size_y + y
            turned = rolled(planes[x][y].astype(F32), 4 * j + 2, 1)
            tile = jnp.where((lane >= 4 * j) & (lane < 4 * j + 4), turned, tile)
    tile = tile.astype(BF16)
    for s in range(1, count_z):
        message = messages[s - 1]
        message[:chans] = tile
        base = chans
        for part in halves(parts[s]) + halves(beside(s)):
            message[base : base + group] = part
            base += group


def pack_y_body(count_y, count_z, size_x, *refs):
    planes = refs[:size_x]
    own = refs[size_x]
    received = refs[size_x + 1 : size_x + count_z]
    outs = refs[size_x + count_z :]
    size_y, chans, size_z = planes[0].shape
    group = own.shape[0] // 2
    lane = lanes_of((chans, size_z))
    before = received[0][:chans].astype(F32)
    after = received[-1][:chans].astype(F32)
    tile = jnp.where(lane % 4 < 2, before, after).astype(BF16)
    main, beside = own[:group], own[group:]
    for message in received:
        pieces = [
            message[chans + i * group : chans + (i + 1) * group].astype(F32)
            for i in range(4)
        ]
        main = main + (pieces[0] + pieces[1])
        beside = beside + (pieces[2] + pieces[3])
    tall = count_y * size_y
    width = 16

    def extended(s):
        found = []
        for values in (main, beside):
            for x in range(size_x):
                part = values[x * tall : (x + 1) * tall]
                found.append(rolled(part, 1 - s * size_y, 0)[:width])
        return jnp.concatenate(found, axis=0)

    tile_out, own_out = outs[0], outs[1]
    tile_out[...] = tile
    own_out[...] = extended(0)
    for s in range(1, count_y):
        message = outs[1 + s]
        high, low = halves(extended(s))
        depth = high.shape[0]
        message[:depth] = high
        message[depth : 2 * depth] = low
        base = 2 * depth
        if s in (1, count_y - 1):
            message[base : base + chans] = tile
            base += chans
            first = size_y - 2 if s == 1 else 0
            for x in range(size_x):
                for y in range(first, first + 2):
                    message[base : base + chans] = planes[x][y]
                    base += chans


def pack_x_body(count_y, size_x, size_y, chans, tile, own, *refs):
    received = refs[: count_y - 1]
    dens, outs = refs[count_y - 1], refs[count_y:]
    depth = own.shape[0]
    total = own[...]
    for message in received:
        total = total + (
            message[:depth].astype(F32) + message[depth : 2 * depth].astype(F32)
        )
    dens[...] = total
    base = 2 * depth
    below, above = received[0], received[-1]
    size_z = tile.shape[1]
    lane = lanes_of((chans, size_z))
    mine = tile[...].astype(F32)
    low = below[base : base + chans].astype(F32)
    high = above[base : base + chans].astype(F32)
    base += chans
    for x in range(size_x):
        first = 4 * x * size_y
        edge = rolled(low, -(first + 4 * (size_y - 2)), 1)
        edge = jnp.where(lane < 8, edge, rolled(mine, 8 - first, 1))
        edge = jnp.where(
            lane < 8 + 4 * size_y, edge, rolled(high, 8 + 4 * size_y - first, 1)
        )
        out = outs[x]
        out[:chans] = edge.astype(BF16)
        start = base + 2 * x * chans
        out[chans : 3 * chans] = below[start : start + 2 * chans]
        out[3 * chans : 5 * chans] = above[start : start + 2 * chans]


def spread(tile, y, width, start):
    lane = lanes_of(tile.shape)
    size = tile.shape[1]
    turned = rolled(tile, size - 2 - 4 * y, 1)
    keep = (lane < 2) | (lane >= size - 2)
    return jnp.where(keep, turned, 0.0).astype(BF16)


def activate(values):
    return jnp.where(values >= 0, values, 0.2 * values) * jnp.sqrt(jnp.float32(2.0))


def column(stack, weights, columns, density, x, y, chans):
    taps = stack[pl.ds(x, 3), pl.ds(y, 3)]
    wide = taps.shape[-1]
    taps = taps.reshape(9 * chans, wide)
    found = jnp.dot(weights[...], taps, preferred_element_type=F32)
    summed = (
        pltpu.roll(found[:chans], 1, 1)
        + found[chans : 2 * chans]
        + pltpu.roll(found[2 * chans :], wide - 1, 1)
    )
    gain = jnp.concatenate([columns[1], columns[1]], axis=1)
    bias = jnp.concatenate([columns[0], columns[0]], axis=1)
    return activate(summed + gain * density + bias)


def first_body(size_x, size_y, *refs):
    own = refs[:size_x]
    edges = refs[size_x : 2 * size_x]
    main_below, main_above, edge_below, edge_above = refs[2 * size_x : 2 * size_x + 4]
    dens, weights, columns = refs[2 * size_x + 4 : 2 * size_x + 7]
    hidden, low_out, high_out, stack, dense, tiles = refs[2 * size_x + 7 :]
    chans, size_z = own[0].shape[1:]
    tall = size_y + 4
    planes = (
        [(main_below, edge_below)] + list(zip(own, edges)) + [(main_above, edge_above)]
    )
    for at, (main, edge) in enumerate(planes):
        stack[at, 2 : 2 + size_y, :, :size_z] = main[...]
        tile = edge[:chans].astype(F32)
        for i, y in enumerate((0, 1, tall - 2, tall - 1)):
            stack[at, y, :, :size_z] = edge[(1 + i) * chans : (2 + i) * chans]
        for y in range(tall):
            stack[at, y, :, size_z:] = spread(tile, y, size_z, 0)
    width = 16
    for x in range(size_x):
        dense[x * width : (x + 1) * width, :size_z] = dens[x * width : (x + 1) * width]
        other = (size_x + x) * width
        dense[x * width : (x + 1) * width, size_z:] = dens[other : other + width]
    lane = lanes_of((chans, size_z))
    for x in range(size_x):
        tiles[...] = jnp.zeros_like(tiles)

        def step(y, carry):
            density = dense[pl.ds(x * width + y, 1), :]
            found = column(stack, weights, columns, density, x, y, chans).astype(BF16)
            hidden[x, y] = found
            beside = found[:, size_z:].astype(F32)
            turned = pltpu.roll(beside, 4 * y + 2, 1)
            keep = (lane >= 4 * y) & (lane < 4 * y + 4)
            tiles[...] = jnp.where(keep, turned, tiles[...])
            return carry

        lax.fori_loop(0, size_y + 2, step, 0)
        out = {0: low_out, size_x - 1: high_out}.get(x)
        if out is not None:
            out[:chans] = tiles[...].astype(BF16)
            for y in range(size_y + 2):
                out[(1 + y) * chans : (2 + y) * chans] = hidden[x, y, :, :size_z]


def second_body(size_x, size_y, hidden, below, above, dens, weights, columns, *refs):
    out, stack, dense, turned = refs
    chans = hidden.shape[2]
    size_z = hidden.shape[3] // 2
    tall = size_y + 2
    stack[1 : 1 + size_x] = hidden[...]
    for at, message in ((0, below), (size_x + 1, above)):
        tile = message[:chans].astype(F32)
        for y in range(tall):
            stack[at, y, :, :size_z] = message[(1 + y) * chans : (2 + y) * chans]
            stack[at, y, :, size_z:] = spread(tile, y, size_z, 0)
    width = 16
    for x in range(size_x):
        dense[x * width : (x + 1) * width, :size_z] = dens[x * width : (x + 1) * width]
        dense[x * width : (x + 1) * width, size_z:] = jnp.zeros((width, size_z), F32)
    for x in range(size_x):

        def step(y, carry):
            density = dense[pl.ds(x * width + y + 1, 1), :]
            found = column(stack, weights, columns, density, x, y, chans)
            turned[y] = found[:, :size_z]
            return carry

        lax.fori_loop(0, size_y, step, 0)
        out[:, x] = jnp.swapaxes(turned[...], 0, 1).astype(BF16)


def shards(
    features,
    dest_bricks,
    cell_ids,
    cic_masses,
    live_counts,
    style_vector,
    affine_first,
    kernel_first,
    bias_first,
    gain_first,
    affine_second,
    kernel_second,
    bias_second,
    gain_second,
):
    chans, size_x, size_y, size_z = features.shape
    count_y, count_z = lax.axis_size("gy"), lax.axis_size("gz")
    group = size_x * count_y * size_y
    depth = 2 * size_x * 16
    planes = call(
        split_body, [((size_y, chans, size_z), BF16)] * size_x, "split"
    )(features)
    main_below = shift(planes[-1], "gx", 1)
    main_above = shift(planes[0], "gx", -1)
    where = jnp.stack([lax.axis_index("gy"), lax.axis_index("gz")]).astype(jnp.int32)
    painted = call(
        functools.partial(paint_body, range(size_x), (count_y, count_z)),
        [((chans + 4 * group, size_z), BF16)] * (count_z - 1)
        + [((2 * group, size_z), F32)],
        "paint",
        smem=(0, 1),
    )(where, live_counts, dest_bricks, cell_ids, cic_masses, *planes)
    from_z = [shift(painted[s - 1], "gz", s) for s in range(1, count_z)]
    rows = [
        2 * depth + ((1 + 2 * size_x) * chans if s in (1, count_y - 1) else 0)
        for s in range(1, count_y)
    ]
    packed = call(
        functools.partial(pack_y_body, count_y, count_z, size_x),
        [((chans, size_z), BF16), ((depth, size_z), F32)]
        + [((r, size_z), BF16) for r in rows],
        "pack_y",
    )(*planes, painted[-1], *from_z)
    from_y = [shift(packed[1 + s], "gy", s) for s in range(1, count_y)]
    weights = []
    for args in (
        (affine_first, kernel_first, bias_first, gain_first),
        (affine_second, kernel_second, bias_second, gain_second),
    ):
        affine, kernel, bias, gain = args
        weights.append(
            call(
                modulate_body,
                [((3 * chans, 9 * chans), BF16), ((2, chans, size_z), F32)],
                "modulate",
            )(
                style_vector[None, :],
                affine,
                kernel,
                bias[None, :],
                gain[None, :],
            )
        )
    edges = call(
        functools.partial(pack_x_body, count_y, size_x, size_y, chans),
        [((depth, size_z), F32)] + [((5 * chans, size_z), BF16)] * size_x,
        "pack_x",
    )(packed[0], packed[1], *from_y)
    dens, edges = edges[0], edges[1:]
    edge_below = shift(edges[-1], "gx", 1)
    edge_above = shift(edges[0], "gx", -1)
    flops = 2 * 27 * chans * chans * 2 * size_z
    hidden, low, high = call(
        functools.partial(first_body, size_x, size_y),
        [
            ((size_x, size_y + 2, chans, 2 * size_z), BF16),
            (((size_y + 3) * chans, size_z), BF16),
            (((size_y + 3) * chans, size_z), BF16),
        ],
        "first",
        flops=flops * size_x * (size_y + 2),
        scratch=[
            pltpu.VMEM((size_x + 2, size_y + 4, chans, 2 * size_z), BF16),
            pltpu.VMEM((size_x * 16, 2 * size_z), F32),
            pltpu.VMEM((chans, size_z), F32),
        ],
    )(
        *planes,
        *edges,
        main_below,
        main_above,
        edge_below,
        edge_above,
        dens,
        *weights[0],
    )
    hidden_below = shift(high, "gx", 1)
    hidden_above = shift(low, "gx", -1)
    (result,) = call(
        functools.partial(second_body, size_x, size_y),
        [((chans, size_x, size_y, size_z), BF16)],
        "second",
        flops=flops * size_x * size_y,
        scratch=[
            pltpu.VMEM((size_x + 2, size_y + 2, chans, 2 * size_z), BF16),
            pltpu.VMEM((size_x * 16, 2 * size_z), F32),
            pltpu.VMEM((size_y, chans, size_z), F32),
        ],
    )(hidden, hidden_below, hidden_above, dens, *weights[1])
    return result


def solution(mesh):
    return jax.shard_map(
        shards,
        mesh=mesh,
        in_specs=(
            P(None, "gx", "gy", "gz"),
            P(("gx", "gy", "gz"), None),
            P(("gx", "gy", "gz"), None),
            P(("gx", "gy", "gz"), None),
            P(("gx", "gy", "gz")),
        )
        + (P(),) * 9,
        out_specs=P(None, "gx", "gy", "gz"),
        check_vma=False,
    )
```

```python
import functools

import jax
import jax.numpy as jnp
from jax import lax
from jax.experimental import pallas as pl
from jax.experimental.pallas import tpu as pltpu
from jax.sharding import PartitionSpec as P

F32 = jnp.float32
BF16 = jnp.bfloat16


def shift(cells, axis, step):
    count = lax.axis_size(axis)
    return lax.ppermute(cells, axis, [(i, (i + step) % count) for i in range(count)])


def call(body, outs, name, flops=0, scratch=(), limit=12):
    def run(*args):
        size = sum(a.size * a.dtype.itemsize for a in args)
        specs = [pl.BlockSpec(memory_space=pltpu.VMEM) for _ in args]
        return pl.pallas_call(
            body,
            out_shape=tuple(jax.ShapeDtypeStruct(s, d) for s, d in outs),
            in_specs=specs,
            out_specs=tuple(pl.BlockSpec(memory_space=pltpu.VMEM) for _ in outs),
            scratch_shapes=list(scratch),
            name=name,
            compiler_params=pltpu.CompilerParams(vmem_limit_bytes=limit << 20),
            cost_estimate=pl.CostEstimate(
                flops=flops, bytes_accessed=size, transcendentals=0
            ),
        )(*args)

    return run


def lanes_of(shape):
    return lax.broadcasted_iota(jnp.int32, shape, len(shape) - 1)


def rolled(values, amount, axis):
    amount = amount % values.shape[axis]
    return values if amount == 0 else pltpu.roll(values, amount, axis)


def halves(values):
    high = values.astype(BF16)
    return high, (values - high.astype(F32)).astype(BF16)


def column_of(row):
    size = row.shape[1]
    wide = jnp.broadcast_to(row, (size, size))
    same = lax.broadcasted_iota(jnp.int32, (size, size), 0) == lanes_of((size, size))
    return jnp.sum(jnp.where(same, wide, jnp.zeros_like(wide)), axis=1, keepdims=True)


def modulate_body(style, *refs):
    for layer in range(2):
        affine, kernel, bias, gain = refs[4 * layer : 4 * layer + 4]
        weights, columns = refs[8 + 2 * layer : 10 + 2 * layer]
        styles = (
            lax.dot_general(
                style[...],
                affine[...],
                (((1,), (1,)), ((), ())),
                precision=lax.Precision.HIGHEST,
                preferred_element_type=F32,
            )
            + 1.0
        )
        chans = kernel.shape[1]
        total = jnp.zeros((chans, kernel.shape[2]), F32)
        for k in range(27):
            scaled = kernel[k].astype(F32) * styles
            total = total + scaled * scaled
        demod = lax.rsqrt(jnp.sum(total, axis=1, keepdims=True) + 1e-08)
        for g in range(3):
            blocks = [
                (kernel[3 * j + g].astype(F32) * styles * demod).astype(BF16)
                for j in range(9)
            ]
            weights[g * chans : (g + 1) * chans, :] = jnp.concatenate(blocks, axis=1)
        columns[0] = jnp.broadcast_to(column_of(bias[...]), columns.shape[1:])
        columns[1] = jnp.broadcast_to(column_of(gain[...]), columns.shape[1:])


def paint_body(count_y, count_z, features, live, dest, cells, masses, *refs):
    size_x = features.shape[1]
    planes, messages, own = refs[:size_x], refs[size_x:-1], refs[-1]
    for at, plane in enumerate(planes):
        part = features[:, at].astype(F32)
        plane[...] = jnp.swapaxes(part, 0, 1).astype(BF16)
    size_y, chans, size_z = planes[0].shape
    blocks, per = cells.shape
    half = blocks // 2
    rank_y, rank_z = lax.axis_index("gy"), lax.axis_index("gz")
    shape = (blocks, per)
    target = jnp.broadcast_to(column_of(dest[...]), shape)
    to_y = lax.div(target, jnp.full(shape, count_z, jnp.int32))
    to_z = target - to_y * count_z - rank_z
    to_y = to_y - rank_y
    to_y = jnp.where(to_y < 0, to_y + count_y, to_y)
    to_z = jnp.where(to_z < 0, to_z + count_z, to_z)
    cell = cells[...]
    cell_row = lax.div(cell, jnp.full(shape, size_z, jnp.int32))
    at_z = cell - cell_row * size_z
    at_x = lax.div(cell_row, jnp.full(shape, size_y, jnp.int32))
    at_y = cell_row - at_x * size_y
    row = ((to_z * size_x + at_x) * count_y + to_y) * size_y + at_y
    alive = lax.broadcasted_iota(jnp.int32, shape, 0) < jnp.broadcast_to(live[...], shape)
    mass = jnp.where(alive, masses[...].astype(F32), 0.0)

    def paired(values):
        return jnp.concatenate([values[:half], values[half:]], axis=1)

    row, at_z, mass = paired(row), paired(at_z), paired(mass)
    width = 2 * per
    group = size_x * count_y * size_y
    total = count_z * group
    iota_rows = lax.broadcasted_iota(jnp.int32, (total, width), 0)
    iota_z = lax.broadcasted_iota(jnp.int32, (size_z, width), 0)
    left, right = [], []
    for r in range(half):
        left.append(
            jnp.where(iota_rows == row[r : r + 1], mass[r : r + 1], 0.0).astype(BF16)
        )
        right.append(jnp.where(iota_z == at_z[r : r + 1], 1.0, 0.0).astype(BF16))
    painted = lax.dot_general(
        jnp.concatenate(left, axis=1),
        jnp.concatenate(right, axis=1),
        (((1,), (1,)), ((), ())),
        preferred_element_type=F32,
    )
    parts = [painted[s * group : (s + 1) * group] for s in range(count_z)]
    lane = lanes_of((group, size_z))

    def beside(s):
        after = parts[(s + 1) % count_z]
        before = parts[(s - 1) % count_z]
        return jnp.where(lane == 0, after, jnp.where(lane == size_z - 1, before, 0.0))

    own[:group] = parts[0]
    own[group:] = beside(0)
    lane = lanes_of((chans, size_z))
    tile = jnp.zeros((chans, size_z), F32)
    for x in range(size_x):
        for y in range(size_y):
            j = x * size_y + y
            turned = rolled(planes[x][y].astype(F32), 4 * j + 2, 1)
            tile = jnp.where((lane >= 4 * j) & (lane < 4 * j + 4), turned, tile)
    tile = tile.astype(BF16)
    for s in range(1, count_z):
        message = messages[s - 1]
        message[:chans] = tile
        base = chans
        for part in halves(parts[s]) + halves(beside(s)):
            message[base : base + group] = part
            base += group


def pack_y_body(count_y, count_z, size_x, *refs):
    planes = refs[:size_x]
    own = refs[size_x]
    received = refs[size_x + 1 : size_x + count_z]
    outs = refs[size_x + count_z :]
    size_y, chans, size_z = planes[0].shape
    group = own.shape[0] // 2
    lane = lanes_of((chans, size_z))
    before = received[0][:chans].astype(F32)
    after = received[-1][:chans].astype(F32)
    tile = jnp.where(lane % 4 < 2, before, after).astype(BF16)
    main, beside = own[:group], own[group:]
    for message in received:
        pieces = [
            message[chans + i * group : chans + (i + 1) * group].astype(F32)
            for i in range(4)
        ]
        main = main + (pieces[0] + pieces[1])
        beside = beside + (pieces[2] + pieces[3])
    tall = count_y * size_y
    width = 16

    def extended(s):
        found = []
        for values in (main, beside):
            for x in range(size_x):
                part = values[x * tall : (x + 1) * tall]
                found.append(rolled(part, 1 - s * size_y, 0)[:width])
        return jnp.concatenate(found, axis=0)

    tile_out, own_out = outs[0], outs[1]
    tile_out[...] = tile
    own_out[...] = extended(0)
    for s in range(1, count_y):
        message = outs[1 + s]
        high, low = halves(extended(s))
        depth = high.shape[0]
        message[:depth] = high
        message[depth : 2 * depth] = low
        base = 2 * depth
        if s in (1, count_y - 1):
            message[base : base + chans] = tile
            base += chans
            first = size_y - 2 if s == 1 else 0
            for x in range(size_x):
                for y in range(first, first + 2):
                    message[base : base + chans] = planes[x][y]
                    base += chans


def pack_x_body(count_y, size_x, size_y, chans, tile, own, *refs):
    received = refs[: count_y - 1]
    dens, outs = refs[count_y - 1], refs[count_y:]
    depth = own.shape[0]
    total = own[...]
    for message in received:
        total = total + (
            message[:depth].astype(F32) + message[depth : 2 * depth].astype(F32)
        )
    dens[...] = total
    base = 2 * depth
    below, above = received[0], received[-1]
    size_z = tile.shape[1]
    lane = lanes_of((chans, size_z))
    mine = tile[...].astype(F32)
    low = below[base : base + chans].astype(F32)
    high = above[base : base + chans].astype(F32)
    base += chans
    for x in range(size_x):
        first = 4 * x * size_y
        edge = rolled(low, -(first + 4 * (size_y - 2)), 1)
        edge = jnp.where(lane < 8, edge, rolled(mine, 8 - first, 1))
        edge = jnp.where(
            lane < 8 + 4 * size_y, edge, rolled(high, 8 + 4 * size_y - first, 1)
        )
        out = outs[x]
        out[:chans] = edge.astype(BF16)
        start = base + 2 * x * chans
        out[chans : 3 * chans] = below[start : start + 2 * chans]
        out[3 * chans : 5 * chans] = above[start : start + 2 * chans]


def spread(tile, y, width, start):
    lane = lanes_of(tile.shape)
    size = tile.shape[1]
    turned = rolled(tile, size - 2 - 4 * y, 1)
    keep = (lane < 2) | (lane >= size - 2)
    return jnp.where(keep, turned, 0.0).astype(BF16)


def activate(values):
    return jnp.where(values >= 0, values, 0.2 * values) * jnp.sqrt(jnp.float32(2.0))


def column(stack, weights, columns, density, x, y, chans):
    taps = stack[pl.ds(x, 3), pl.ds(y, 3)]
    wide = taps.shape[-1]
    taps = taps.reshape(9 * chans, wide)
    found = jnp.dot(weights[...], taps, preferred_element_type=F32)
    summed = (
        pltpu.roll(found[:chans], 1, 1)
        + found[chans : 2 * chans]
        + pltpu.roll(found[2 * chans :], wide - 1, 1)
    )
    gain = jnp.concatenate([columns[1], columns[1]], axis=1)
    bias = jnp.concatenate([columns[0], columns[0]], axis=1)
    return activate(summed + gain * density + bias)


def first_body(size_x, size_y, *refs):
    own = refs[:size_x]
    edges = refs[size_x : 2 * size_x]
    main_below, main_above, edge_below, edge_above = refs[2 * size_x : 2 * size_x + 4]
    dens, weights, columns = refs[2 * size_x + 4 : 2 * size_x + 7]
    hidden, low_out, high_out, stack, dense, tiles = refs[2 * size_x + 7 :]
    chans, size_z = own[0].shape[1:]
    tall = size_y + 4
    planes = (
        [(main_below, edge_below)] + list(zip(own, edges)) + [(main_above, edge_above)]
    )
    for at, (main, edge) in enumerate(planes):
        stack[at, 2 : 2 + size_y, :, :size_z] = main[...]
        tile = edge[:chans].astype(F32)
        for i, y in enumerate((0, 1, tall - 2, tall - 1)):
            stack[at, y, :, :size_z] = edge[(1 + i) * chans : (2 + i) * chans]
        for y in range(tall):
            stack[at, y, :, size_z:] = spread(tile, y, size_z, 0)
    width = 16
    for x in range(size_x):
        dense[x * width : (x + 1) * width, :size_z] = dens[x * width : (x + 1) * width]
        other = (size_x + x) * width
        dense[x * width : (x + 1) * width, size_z:] = dens[other : other + width]
    lane = lanes_of((chans, size_z))
    for x in range(size_x):
        tiles[...] = jnp.zeros_like(tiles)

        def step(y, carry):
            density = dense[pl.ds(x * width + y, 1), :]
            found = column(stack, weights, columns, density, x, y, chans).astype(BF16)
            hidden[x, y] = found
            beside = found[:, size_z:].astype(F32)
            turned = pltpu.roll(beside, 4 * y + 2, 1)
            keep = (lane >= 4 * y) & (lane < 4 * y + 4)
            tiles[...] = jnp.where(keep, turned, tiles[...])
            return carry

        [step(y, 0) for y in range(size_y + 2)]
        out = {0: low_out, size_x - 1: high_out}.get(x)
        if out is not None:
            out[:chans] = tiles[...].astype(BF16)
            for y in range(size_y + 2):
                out[(1 + y) * chans : (2 + y) * chans] = hidden[x, y, :, :size_z]


def second_body(size_x, size_y, hidden, below, above, dens, weights, columns, *refs):
    out, stack, dense, turned = refs
    chans = hidden.shape[2]
    size_z = hidden.shape[3] // 2
    tall = size_y + 2
    stack[1 : 1 + size_x] = hidden[...]
    for at, message in ((0, below), (size_x + 1, above)):
        tile = message[:chans].astype(F32)
        for y in range(tall):
            stack[at, y, :, :size_z] = message[(1 + y) * chans : (2 + y) * chans]
            stack[at, y, :, size_z:] = spread(tile, y, size_z, 0)
    width = 16
    for x in range(size_x):
        dense[x * width : (x + 1) * width, :size_z] = dens[x * width : (x + 1) * width]
        dense[x * width : (x + 1) * width, size_z:] = jnp.zeros((width, size_z), F32)
    for x in range(size_x):

        def step(y, carry):
            density = dense[pl.ds(x * width + y + 1, 1), :]
            found = column(stack, weights, columns, density, x, y, chans)
            turned[y] = found[:, :size_z]
            return carry

        [step(y, 0) for y in range(size_y)]
        out[:, x] = jnp.swapaxes(turned[...], 0, 1).astype(BF16)


def shards(
    features,
    dest_bricks,
    cell_ids,
    cic_masses,
    live_counts,
    style_vector,
    affine_first,
    kernel_first,
    bias_first,
    gain_first,
    affine_second,
    kernel_second,
    bias_second,
    gain_second,
):
    chans, size_x, size_y, size_z = features.shape
    count_y, count_z = lax.axis_size("gy"), lax.axis_size("gz")
    group = size_x * count_y * size_y
    depth = 2 * size_x * 16
    painted = call(
        functools.partial(paint_body, count_y, count_z),
        [((size_y, chans, size_z), BF16)] * size_x
        + [((chans + 4 * group, size_z), BF16)] * (count_z - 1)
        + [((2 * group, size_z), F32)],
        "paint",
    )(features, live_counts[None, :], dest_bricks.T, cell_ids, cic_masses)
    planes, painted = painted[:size_x], painted[size_x:]
    main_below = shift(planes[-1], "gx", 1)
    main_above = shift(planes[0], "gx", -1)
    from_z = [shift(painted[s - 1], "gz", s) for s in range(1, count_z)]
    rows = [
        2 * depth + ((1 + 2 * size_x) * chans if s in (1, count_y - 1) else 0)
        for s in range(1, count_y)
    ]
    packed = call(
        functools.partial(pack_y_body, count_y, count_z, size_x),
        [((chans, size_z), BF16), ((depth, size_z), F32)]
        + [((r, size_z), BF16) for r in rows],
        "pack_y",
    )(*planes, painted[-1], *from_z)
    from_y = [shift(packed[1 + s], "gy", s) for s in range(1, count_y)]
    modulated = call(
        modulate_body,
        [((3 * chans, 9 * chans), BF16), ((2, chans, size_z), F32)] * 2,
        "modulate",
        flops=1 << 22,
    )(
        style_vector[None, :],
        affine_first.T,
        kernel_first,
        bias_first[None, :],
        gain_first[None, :],
        affine_second.T,
        kernel_second,
        bias_second[None, :],
        gain_second[None, :],
    )
    edges = call(
        functools.partial(pack_x_body, count_y, size_x, size_y, chans),
        [((depth, size_z), F32)] + [((5 * chans, size_z), BF16)] * size_x,
        "pack_x",
    )(packed[0], packed[1], *from_y)
    dens, edges = edges[0], edges[1:]
    edge_below = shift(edges[-1], "gx", 1)
    edge_above = shift(edges[0], "gx", -1)
    flops = 2 * 27 * chans * chans * 2 * size_z
    hidden, low, high = call(
        functools.partial(first_body, size_x, size_y),
        [
            ((size_x, size_y + 2, chans, 2 * size_z), BF16),
            (((size_y + 3) * chans, size_z), BF16),
            (((size_y + 3) * chans, size_z), BF16),
        ],
        "first",
        limit=24,
        flops=flops * size_x * (size_y + 2),
        scratch=[
            pltpu.VMEM((size_x + 2, size_y + 4, chans, 2 * size_z), BF16),
            pltpu.VMEM((size_x * 16, 2 * size_z), F32),
            pltpu.VMEM((chans, size_z), F32),
        ],
    )(
        *planes,
        *edges,
        main_below,
        main_above,
        edge_below,
        edge_above,
        dens,
        *modulated[:2],
    )
    hidden_below = shift(high, "gx", 1)
    hidden_above = shift(low, "gx", -1)
    (result,) = call(
        functools.partial(second_body, size_x, size_y),
        [((chans, size_x, size_y, size_z), BF16)],
        "second",
        limit=24,
        flops=flops * size_x * size_y,
        scratch=[
            pltpu.VMEM((size_x + 2, size_y + 2, chans, 2 * size_z), BF16),
            pltpu.VMEM((size_x * 16, 2 * size_z), F32),
            pltpu.VMEM((size_y, chans, size_z), F32),
        ],
    )(hidden, hidden_below, hidden_above, dens, *modulated[2:])
    return result


def solution(mesh):
    return jax.shard_map(
        shards,
        mesh=mesh,
        in_specs=(
            P(None, "gx", "gy", "gz"),
            P(("gx", "gy", "gz"), None),
            P(("gx", "gy", "gz"), None),
            P(("gx", "gy", "gz"), None),
            P(("gx", "gy", "gz")),
        )
        + (P(),) * 9,
        out_specs=P(None, "gx", "gy", "gz"),
        check_vma=False,
    )
```

```python
import functools

import jax
import jax.numpy as jnp
from jax import lax
from jax.experimental import pallas as pl
from jax.experimental.pallas import tpu as pltpu
from jax.sharding import PartitionSpec as P


F32 = jnp.float32
BF16 = jnp.bfloat16


def shift(cells, axis, step):
    count = lax.axis_size(axis)
    pairs = [(i, (i + step) % count) for i in range(count)]
    return lax.ppermute(cells, axis, pairs)


def call(body, outs, flops=0, scratch=(), limit=12, fetched=()):
    def run(*args):
        size = sum(a.size * a.dtype.itemsize for a in args)
        specs = [
            pl.BlockSpec(memory_space=pltpu.HBM if i in fetched else pltpu.VMEM)
            for i in range(len(args))
        ]
        buffers = [pltpu.VMEM(args[i].shape, args[i].dtype) for i in fetched]
        extra = [pltpu.SemaphoreType.DMA((len(fetched),))] if fetched else []

        def wrapped(*refs):
            refs = list(refs)
            if fetched:
                done = refs.pop()
                held = refs[-len(fetched) :]
                refs = refs[: -len(fetched)]
                copies = [
                    pltpu.make_async_copy(refs[i], held[at], done.at[at])
                    for at, i in enumerate(fetched)
                ]
                for copy in copies:
                    copy.start()
                for copy in copies:
                    copy.wait()
                for at, i in enumerate(fetched):
                    refs[i] = held[at]
            body(*refs)

        kernel = pl.pallas_call(
            wrapped,
            out_shape=tuple(jax.ShapeDtypeStruct(s, d) for s, d in outs),
            in_specs=specs,
            out_specs=tuple(pl.BlockSpec(memory_space=pltpu.VMEM) for _ in outs),
            scratch_shapes=list(scratch) + buffers + extra,
            compiler_params=pltpu.CompilerParams(vmem_limit_bytes=limit << 20),
            cost_estimate=pl.CostEstimate(
                flops=flops, bytes_accessed=size, transcendentals=0
            ),
        )
        args = [
            pltpu.with_memory_space_constraint(a, pltpu.HBM) if i in fetched else a
            for i, a in enumerate(args)
        ]
        return kernel(*args)

    return run


def lanes_of(shape):
    return lax.broadcasted_iota(jnp.int32, shape, len(shape) - 1)


def rolled(values, amount, axis):
    amount = amount % values.shape[axis]
    return values if amount == 0 else pltpu.roll(values, amount, axis)


def ends(values, base):
    lane = lanes_of(values.shape)
    high = rolled(values, -(base + 1), 1)
    low = rolled(values, -(base + 3), 1)
    return jnp.where((lane == 0) | (lane == values.shape[1] - 1), high + low, 0.0)


def with_ends(tile, values, base):
    lane = lanes_of(tile.shape)
    high, low = (part.astype(F32) for part in halves(values))
    tile = jnp.where(
        (lane == base) | (lane == base + 1), rolled(high, base + 1, 1), tile
    )
    return jnp.where(
        (lane == base + 2) | (lane == base + 3), rolled(low, base + 3, 1), tile
    )


def halves(values):
    high = values.astype(BF16)
    return high, (values - high.astype(F32)).astype(BF16)


def store_halves(message, start, values):
    size = values.shape[0]
    message[start : start + size], message[start + size : start + 2 * size] = halves(
        values
    )


def load_halves(message, start, size):
    return message[start : start + size].astype(F32) + message[
        start + size : start + 2 * size
    ].astype(F32)


def column_of(row):
    size = row.shape[1]
    wide = jnp.broadcast_to(row, (size, size))
    same = lax.broadcasted_iota(jnp.int32, (size, size), 0) == lanes_of((size, size))
    return jnp.sum(jnp.where(same, wide, jnp.zeros_like(wide)), axis=1, keepdims=True)


def modulate_body(style, *refs):
    for layer in range(2):
        affine, kernel, bias, gain = refs[4 * layer : 4 * layer + 4]
        weights, columns = refs[8 + 2 * layer : 10 + 2 * layer]
        styles = (
            lax.dot_general(
                style[...],
                affine[...],
                (((1,), (1,)), ((), ())),
                precision=lax.Precision.HIGHEST,
                preferred_element_type=F32,
            )
            + 1.0
        )
        chans = kernel.shape[1]
        total = jnp.zeros((chans, kernel.shape[2]), F32)
        for k in range(27):
            scaled = kernel[k].astype(F32) * styles
            total = total + scaled * scaled
        demod = lax.rsqrt(jnp.sum(total, axis=1, keepdims=True) + 1e-08)
        for g in range(3):
            blocks = [
                (kernel[3 * j + g].astype(F32) * styles * demod).astype(BF16)
                for j in range(9)
            ]
            weights[g * chans : (g + 1) * chans, :] = jnp.concatenate(blocks, axis=1)
        columns[0] = jnp.broadcast_to(column_of(bias[...]), columns.shape[1:])
        columns[1] = jnp.broadcast_to(column_of(gain[...]), columns.shape[1:])


def paint_body(count_y, count_z, features, live, dest, cells, masses, *refs):
    size_x = features.shape[1]
    planes, messages, own = refs[0], refs[1:-1], refs[-1]
    for at in range(size_x):
        part = features[:, at].astype(F32)
        planes[at] = jnp.swapaxes(part, 0, 1).astype(BF16)
    size_y, chans, size_z = planes.shape[1:]
    blocks, per = cells.shape
    half = blocks // 2
    rank_y, rank_z = lax.axis_index("gy"), lax.axis_index("gz")
    shape = (blocks, per)
    target = jnp.broadcast_to(column_of(dest[...]), shape)
    to_y = lax.div(target, jnp.full(shape, count_z, jnp.int32))
    to_z = target - to_y * count_z - rank_z
    to_y = to_y - rank_y
    to_y = jnp.where(to_y < 0, to_y + count_y, to_y)
    to_z = jnp.where(to_z < 0, to_z + count_z, to_z)
    cell = cells[...]
    cell_row = lax.div(cell, jnp.full(shape, size_z, jnp.int32))
    at_z = cell - cell_row * size_z
    at_x = lax.div(cell_row, jnp.full(shape, size_y, jnp.int32))
    at_y = cell_row - at_x * size_y
    row = ((to_z * size_x + at_x) * count_y + to_y) * size_y + at_y
    alive = lax.broadcasted_iota(jnp.int32, shape, 0) < jnp.broadcast_to(live[...], shape)
    mass = jnp.where(alive, masses[...].astype(F32), 0.0)

    def paired(values):
        return jnp.concatenate([values[:half], values[half:]], axis=1)

    row, at_z, mass = paired(row), paired(at_z), paired(mass)
    width = 2 * per
    group = size_x * count_y * size_y
    total = count_z * group
    iota_rows = lax.broadcasted_iota(jnp.int32, (total, width), 0)
    iota_z = lax.broadcasted_iota(jnp.int32, (size_z, width), 0)
    left, right = [], []
    for r in range(half):
        left.append(
            jnp.where(iota_rows == row[r : r + 1], mass[r : r + 1], 0.0).astype(BF16)
        )
        right.append(jnp.where(iota_z == at_z[r : r + 1], 1.0, 0.0).astype(BF16))
    painted = lax.dot_general(
        jnp.concatenate(left, axis=1),
        jnp.concatenate(right, axis=1),
        (((1,), (1,)), ((), ())),
        preferred_element_type=F32,
    )
    parts = [painted[s * group : (s + 1) * group] for s in range(count_z)]
    lane = lanes_of((group, size_z))

    def beside(s):
        after = parts[(s + 1) % count_z]
        before = parts[(s - 1) % count_z]
        return jnp.where(lane == 0, after, jnp.where(lane == size_z - 1, before, 0.0))

    own[:group] = parts[0]
    own[group:] = beside(0)
    lane = lanes_of((chans, size_z))
    tile = jnp.zeros((chans, size_z), F32)
    for x in range(size_x):
        for y in range(size_y):
            j = x * size_y + y
            turned = rolled(planes[x, y].astype(F32), 4 * j + 2, 1)
            tile = jnp.where((lane >= 4 * j) & (lane < 4 * j + 4), turned, tile)
    base = 4 * size_x * size_y
    for s in range(1, count_z):
        message = messages[s - 1]
        message[:chans] = with_ends(tile, beside(s), base).astype(BF16)
        store_halves(message, chans, parts[s])


def pack_y_body(count_y, count_z, size_x, *refs):
    planes, own = refs[:2]
    received = refs[2 : 1 + count_z]
    outs = refs[1 + count_z :]
    size_y, chans, size_z = planes.shape[1:]
    group = own.shape[0] // 2
    lane = lanes_of((chans, size_z))
    before = received[0][:chans].astype(F32)
    after = received[-1][:chans].astype(F32)
    tile = jnp.where(lane % 4 < 2, before, after)
    base = 4 * size_x * size_y
    main, beside = own[:group], own[group:]
    for message in received:
        main = main + load_halves(message, chans, group)
        beside = beside + ends(message[:chans].astype(F32), base)
    tall = count_y * size_y
    width = 16

    def extended(s, values):
        found = []
        for x in range(size_x):
            part = values[x * tall : (x + 1) * tall]
            found.append(rolled(part, 1 - s * size_y, 0)[:width])
        return jnp.concatenate(found, axis=0)

    tile_out, own_out = outs[0], outs[1]
    tile_out[...] = tile.astype(BF16)
    depth = size_x * width
    own_out[:depth] = extended(0, main)
    own_out[depth:] = extended(0, beside)
    for s in range(1, count_y):
        message = outs[1 + s]
        store_halves(message, 0, extended(s, main))
        edge = extended(s, beside)
        if s not in (1, count_y - 1):
            message[2 * depth :] = with_ends(edge, edge, base).astype(BF16)
            continue
        edge = jnp.concatenate([edge, jnp.zeros((chans - depth, size_z), F32)], axis=0)
        message[2 * depth : 2 * depth + chans] = with_ends(tile, edge, base).astype(BF16)
        at = 2 * depth + chans
        first = size_y - 2 if s == 1 else 0
        for x in range(size_x):
            for y in range(first, first + 2):
                message[at : at + chans] = planes[x, y]
                at += chans


def pack_x_body(count_y, size_x, size_y, chans, tile, own, *refs):
    received = refs[: count_y - 1]
    dens, out = refs[count_y - 1], refs[count_y]
    depth = own.shape[0] // 2
    base = 4 * size_x * size_y
    main, beside = own[:depth], own[depth:]
    for message in received:
        main = main + load_halves(message, 0, depth)
        beside = beside + ends(message[2 * depth : 3 * depth].astype(F32), base)
    dens[:depth] = main
    dens[depth:] = beside
    base = 2 * depth
    below, above = received[0], received[-1]
    size_z = tile.shape[1]
    lane = lanes_of((chans, size_z))
    mine = tile[...].astype(F32)
    low = below[base : base + chans].astype(F32)
    high = above[base : base + chans].astype(F32)
    base += chans
    at = chans
    tall = size_y + 4
    edge = jnp.zeros((chans, size_z), F32)
    for x in range(size_x):
        first = 4 * x * size_y
        to = 4 * x * tall
        edge = jnp.where(
            lane >= to, rolled(low, to - first - 4 * (size_y - 2), 1), edge
        )
        edge = jnp.where(lane >= to + 8, rolled(mine, to + 8 - first, 1), edge)
        edge = jnp.where(
            lane >= to + 8 + 4 * size_y,
            rolled(high, to + 8 + 4 * size_y - first, 1),
            edge,
        )
        start = base + 2 * x * chans
        for message in (below, above):
            out[at : at + 2 * chans] = message[start : start + 2 * chans]
            at += 2 * chans
    beside = jnp.concatenate([beside, jnp.zeros((chans - depth, size_z), F32)], axis=0)
    out[:chans] = with_ends(edge, beside, 4 * size_x * tall).astype(BF16)
    store_halves(out, at, main)


def spread(tile, y):
    lane = lanes_of(tile.shape)
    size = tile.shape[1]
    turned = rolled(tile, size - 2 - 4 * y, 1)
    keep = (lane < 2) | (lane >= size - 2)
    return jnp.where(keep, turned, 0.0).astype(BF16)


def activate(values):
    return jnp.where(values >= 0, values, 0.2 * values) * jnp.sqrt(jnp.float32(2.0))


def column(stack, weights, columns, density, x, y, chans):
    taps = stack[pl.ds(x, 3), pl.ds(y, 3)]
    wide = taps.shape[-1]
    taps = taps.reshape(9 * chans, wide)
    found = jnp.dot(weights[...], taps, preferred_element_type=F32)
    summed = (
        pltpu.roll(found[:chans], 1, 1)
        + found[chans : 2 * chans]
        + pltpu.roll(found[2 * chans :], wide - 1, 1)
    )
    gain = jnp.concatenate([columns[1], columns[1]], axis=1)
    bias = jnp.concatenate([columns[0], columns[0]], axis=1)
    return activate(summed + gain * density + bias)


def both_body(size_x, size_y, *refs):
    own, own_edge, main_below, main_above, edge_below, edge_above, dens = refs[:7]
    first, first_columns, second, second_columns = refs[7:11]
    out, stack, hidden, dense, turned = refs[11:]
    chans, size_z = own.shape[2:]
    tall = size_y + 4
    width = 16
    depth = size_x * width
    sources = [(main_below, edge_below, main_below.shape[0] - 2 + i) for i in range(2)]
    sources += [(own, own_edge, x) for x in range(size_x)]
    sources += [(main_above, edge_above, i) for i in range(2)]
    last = size_x - 1
    for at, (main, edge, x) in enumerate(sources):
        stack[at, 2 : 2 + size_y, :, :size_z] = main[x]
        tile = edge[:chans].astype(F32)
        start = (1 + 4 * x) * chans
        for i, y in enumerate((0, 1, tall - 2, tall - 1)):
            stack[at, y, :, :size_z] = edge[start + i * chans : start + (i + 1) * chans]
        for y in range(tall):
            stack[at, y, :, size_z:] = spread(tile, x * tall + y)
    dense[width : width + depth, :size_z] = dens[:depth]
    dense[width : width + depth, size_z:] = dens[depth:]
    start = (1 + 4 * size_x) * chans
    for edge, x, at in (
        (edge_below, last, 0),
        (edge_above, 0, width + depth),
    ):
        main = load_halves(edge, start, depth)
        beside = ends(edge[:depth].astype(F32), 4 * size_x * tall)
        dense[at : at + width, :size_z] = main[x * width : (x + 1) * width]
        dense[at : at + width, size_z:] = beside[x * width : (x + 1) * width]
    for x in range(size_x + 2):
        for y in range(size_y + 2):
            density = dense[pl.ds(x * width + y, 1), :]
            found = column(stack, first, first_columns, density, x, y, chans)
            hidden[x, y] = found.astype(BF16)
    for x in range(size_x):
        for y in range(size_y):
            density = dense[pl.ds((x + 1) * width + y + 1, 1), :]
            found = column(hidden, second, second_columns, density, x, y, chans)
            turned[y] = found[:, :size_z]
        out[:, x] = jnp.swapaxes(turned[...], 0, 1).astype(BF16)


def shards(
    features,
    dest_bricks,
    cell_ids,
    cic_masses,
    live_counts,
    style_vector,
    affine_first,
    kernel_first,
    bias_first,
    gain_first,
    affine_second,
    kernel_second,
    bias_second,
    gain_second,
):
    chans, size_x, size_y, size_z = features.shape
    count_y, count_z = lax.axis_size("gy"), lax.axis_size("gz")
    group = size_x * count_y * size_y
    assert group == chans and 4 * size_x * (size_y + 4) + 4 <= size_z
    depth = size_x * 16
    painted = call(
        functools.partial(paint_body, count_y, count_z),
        [((size_x, size_y, chans, size_z), BF16)]
        + [((chans + 2 * group, size_z), BF16)] * (count_z - 1)
        + [((2 * group, size_z), F32)],
        fetched=(0, 2, 3, 4),
    )(features, live_counts[None, :], dest_bricks.T, cell_ids, cic_masses)
    planes, painted = painted[0], painted[1:]
    main_below = shift(planes[size_x - 2 :], "gx", 1)
    main_above = shift(planes[:2], "gx", -1)
    from_z = [shift(painted[s - 1], "gz", s) for s in range(1, count_z)]
    rows = [
        2 * depth + ((1 + 2 * size_x) * chans if s in (1, count_y - 1) else depth)
        for s in range(1, count_y)
    ]
    packed = call(
        functools.partial(pack_y_body, count_y, count_z, size_x),
        [((chans, size_z), BF16), ((2 * depth, size_z), F32)]
        + [((r, size_z), BF16) for r in rows],
    )(planes, painted[-1], *from_z)
    from_y = [shift(packed[1 + s], "gy", s) for s in range(1, count_y)]
    modulated = call(
        modulate_body,
        [((3 * chans, 9 * chans), BF16), ((2, chans, size_z), F32)] * 2,
        flops=1 << 22,
        fetched=tuple(range(9)),
    )(
        style_vector[None, :],
        affine_first.T,
        kernel_first,
        bias_first[None, :],
        gain_first[None, :],
        affine_second.T,
        kernel_second,
        bias_second[None, :],
        gain_second[None, :],
    )
    dens, edges = call(
        functools.partial(pack_x_body, count_y, size_x, size_y, chans),
        [
            ((2 * depth, size_z), F32),
            (((1 + 4 * size_x) * chans + 2 * depth, size_z), BF16),
        ],
    )(packed[0], packed[1], *from_y)
    edge_below = shift(edges, "gx", 1)
    edge_above = shift(edges, "gx", -1)
    columns = (size_x + 2) * (size_y + 2) + size_x * size_y
    (result,) = call(
        functools.partial(both_body, size_x, size_y),
        [((chans, size_x, size_y, size_z), BF16)],
        limit=24,
        flops=2 * 27 * chans * chans * 2 * size_z * columns,
        scratch=[
            pltpu.VMEM((size_x + 4, size_y + 4, chans, 2 * size_z), BF16),
            pltpu.VMEM((size_x + 2, size_y + 2, chans, 2 * size_z), BF16),
            pltpu.VMEM(((size_x + 2) * 16, 2 * size_z), F32),
            pltpu.VMEM((size_y, chans, size_z), F32),
        ],
    )(
        planes,
        edges,
        main_below,
        main_above,
        edge_below,
        edge_above,
        dens,
        *modulated,
    )
    return result


def solution(mesh):
    return jax.shard_map(
        shards,
        mesh=mesh,
        in_specs=(
            P(None, "gx", "gy", "gz"),
            P(("gx", "gy", "gz"), None),
            P(("gx", "gy", "gz"), None),
            P(("gx", "gy", "gz"), None),
            P(("gx", "gy", "gz")),
        )
        + (P(),) * 9,
        out_specs=P(None, "gx", "gy", "gz"),
        check_vma=False,
    )
```

```python
import functools

import jax
import jax.numpy as jnp
from jax import lax
from jax.experimental import pallas as pl
from jax.experimental.pallas import tpu as pltpu
from jax.sharding import PartitionSpec as P


F32 = jnp.float32
BF16 = jnp.bfloat16


def shift(cells, axis, step):
    count = lax.axis_size(axis)
    pairs = [(i, (i + step) % count) for i in range(count)]
    return lax.ppermute(cells, axis, pairs)


def call(body, outs, flops=0, scratch=(), limit=12, fetched=(), late=()):
    def run(*args):
        size = sum(a.size * a.dtype.itemsize for a in args)
        specs = [
            pl.BlockSpec(memory_space=pltpu.HBM if i in fetched else pltpu.VMEM)
            for i in range(len(args))
        ]
        buffers = [pltpu.VMEM(args[i].shape, args[i].dtype) for i in fetched]
        extra = [pltpu.SemaphoreType.DMA((len(fetched),))] if fetched else []

        def wrapped(*refs):
            refs = list(refs)
            if fetched:
                done = refs.pop()
                held = refs[-len(fetched) :]
                refs = refs[: -len(fetched)]
                copies = [
                    pltpu.make_async_copy(refs[i], held[at], done.at[at])
                    for at, i in enumerate(fetched)
                ]
                for copy in copies:
                    copy.start()
                for at, i in enumerate(fetched):
                    refs[i] = held[at]
                    if i not in late:
                        copies[at].wait()
                if late:
                    refs.insert(0, [copies[fetched.index(i)] for i in late])
            body(*refs)

        kernel = pl.pallas_call(
            wrapped,
            out_shape=tuple(jax.ShapeDtypeStruct(s, d) for s, d in outs),
            in_specs=specs,
            out_specs=tuple(pl.BlockSpec(memory_space=pltpu.VMEM) for _ in outs),
            scratch_shapes=list(scratch) + buffers + extra,
            compiler_params=pltpu.CompilerParams(vmem_limit_bytes=limit << 20),
            cost_estimate=pl.CostEstimate(
                flops=flops, bytes_accessed=size, transcendentals=0
            ),
        )
        args = [
            pltpu.with_memory_space_constraint(a, pltpu.HBM) if i in fetched else a
            for i, a in enumerate(args)
        ]
        return kernel(*args)

    return run


def lanes_of(shape):
    return lax.broadcasted_iota(jnp.int32, shape, len(shape) - 1)


def rolled(values, amount, axis):
    amount = amount % values.shape[axis]
    return values if amount == 0 else pltpu.roll(values, amount, axis)


def ends(values, base):
    lane = lanes_of(values.shape)
    high = rolled(values, -(base + 1), 1)
    low = rolled(values, -(base + 3), 1)
    return jnp.where((lane == 0) | (lane == values.shape[1] - 1), high + low, 0.0)


def with_ends(tile, values, base):
    lane = lanes_of(tile.shape)
    high, low = (part.astype(F32) for part in halves(values))
    tile = jnp.where(
        (lane == base) | (lane == base + 1), rolled(high, base + 1, 1), tile
    )
    return jnp.where(
        (lane == base + 2) | (lane == base + 3), rolled(low, base + 3, 1), tile
    )


def halves(values):
    high = values.astype(BF16)
    return high, (values - high.astype(F32)).astype(BF16)


def store_halves(message, start, values):
    size = values.shape[0]
    message[start : start + size], message[start + size : start + 2 * size] = halves(
        values
    )


def load_halves(message, start, size):
    return message[start : start + size].astype(F32) + message[
        start + size : start + 2 * size
    ].astype(F32)


def column_of(row):
    size = row.shape[1]
    wide = jnp.broadcast_to(row, (size, size))
    same = lax.broadcasted_iota(jnp.int32, (size, size), 0) == lanes_of((size, size))
    return jnp.sum(jnp.where(same, wide, jnp.zeros_like(wide)), axis=1, keepdims=True)


def modulate_body(style, *refs):
    for layer in range(2):
        affine, kernel, bias, gain = refs[4 * layer : 4 * layer + 4]
        weights, columns = refs[8 + 2 * layer : 10 + 2 * layer]
        styles = (
            lax.dot_general(
                style[...],
                affine[...],
                (((1,), (1,)), ((), ())),
                precision=lax.Precision.HIGHEST,
                preferred_element_type=F32,
            )
            + 1.0
        )
        chans = kernel.shape[1]
        total = jnp.zeros((chans, kernel.shape[2]), F32)
        for k in range(27):
            scaled = kernel[k].astype(F32) * styles
            total = total + scaled * scaled
        demod = lax.rsqrt(jnp.sum(total, axis=1, keepdims=True) + 1e-08)
        for e in range(3):
            for g in range(3):
                blocks = [
                    (kernel[9 * e + 3 * f + g].astype(F32) * styles * demod).astype(
                        BF16
                    )
                    for f in range(3)
                ]
                weights[e, g * chans : (g + 1) * chans, :] = jnp.concatenate(
                    blocks, axis=1
                )
        columns[0] = jnp.broadcast_to(column_of(bias[...]), columns.shape[1:])
        columns[1] = jnp.broadcast_to(column_of(gain[...]), columns.shape[1:])


def paint_body(count_y, count_z, pending, features, live, dest, cells, masses, *refs):
    size_x = features.shape[1]
    planes, messages, own = refs[0], refs[1:-1], refs[-1]
    size_y, chans, size_z = planes.shape[1:]
    blocks, per = cells.shape
    half = blocks // 2
    rank_y, rank_z = lax.axis_index("gy"), lax.axis_index("gz")
    shape = (blocks, per)
    target = jnp.broadcast_to(column_of(dest[...]), shape)
    to_y = lax.div(target, jnp.full(shape, count_z, jnp.int32))
    to_z = target - to_y * count_z - rank_z
    to_y = to_y - rank_y
    to_y = jnp.where(to_y < 0, to_y + count_y, to_y)
    to_z = jnp.where(to_z < 0, to_z + count_z, to_z)
    cell = cells[...]
    cell_row = lax.div(cell, jnp.full(shape, size_z, jnp.int32))
    at_z = cell - cell_row * size_z
    at_x = lax.div(cell_row, jnp.full(shape, size_y, jnp.int32))
    at_y = cell_row - at_x * size_y
    row = ((to_z * size_x + at_x) * count_y + to_y) * size_y + at_y
    alive = lax.broadcasted_iota(jnp.int32, shape, 0) < jnp.broadcast_to(live[...], shape)
    mass = jnp.where(alive, masses[...].astype(F32), 0.0)

    def paired(values):
        return jnp.concatenate([values[:half], values[half:]], axis=1)

    row, at_z, mass = paired(row), paired(at_z), paired(mass)
    width = 2 * per
    group = size_x * count_y * size_y
    total = count_z * group
    iota_rows = lax.broadcasted_iota(jnp.int32, (total, width), 0)
    iota_z = lax.broadcasted_iota(jnp.int32, (size_z, width), 0)
    left, right = [], []
    for r in range(half):
        left.append(
            jnp.where(iota_rows == row[r : r + 1], mass[r : r + 1], 0.0).astype(BF16)
        )
        right.append(jnp.where(iota_z == at_z[r : r + 1], 1.0, 0.0).astype(BF16))
    painted = lax.dot_general(
        jnp.concatenate(left, axis=1),
        jnp.concatenate(right, axis=1),
        (((1,), (1,)), ((), ())),
        preferred_element_type=F32,
    )
    parts = [painted[s * group : (s + 1) * group] for s in range(count_z)]
    lane = lanes_of((group, size_z))

    def beside(s):
        after = parts[(s + 1) % count_z]
        before = parts[(s - 1) % count_z]
        return jnp.where(lane == 0, after, jnp.where(lane == size_z - 1, before, 0.0))

    own[:group] = parts[0]
    own[group:] = beside(0)
    for copy in pending:
        copy.wait()
    for at in range(size_x):
        part = features[:, at].astype(F32)
        planes[at] = jnp.swapaxes(part, 0, 1).astype(BF16)
    lane = lanes_of((chans, size_z))
    tile = jnp.zeros((chans, size_z), F32)
    for x in range(size_x):
        for y in range(size_y):
            j = x * size_y + y
            turned = rolled(planes[x, y].astype(F32), 4 * j + 2, 1)
            tile = jnp.where((lane >= 4 * j) & (lane < 4 * j + 4), turned, tile)
    base = 4 * size_x * size_y
    for s in range(1, count_z):
        message = messages[s - 1]
        message[:chans] = with_ends(tile, beside(s), base).astype(BF16)
        store_halves(message, chans, parts[s])


def pack_y_body(count_y, count_z, size_x, *refs):
    planes, own = refs[:2]
    received = refs[2 : 1 + count_z]
    outs = refs[1 + count_z :]
    size_y, chans, size_z = planes.shape[1:]
    group = own.shape[0] // 2
    lane = lanes_of((chans, size_z))
    before = received[0][:chans].astype(F32)
    after = received[-1][:chans].astype(F32)
    tile = jnp.where(lane % 4 < 2, before, after)
    base = 4 * size_x * size_y
    main, beside = own[:group], own[group:]
    for message in received:
        main = main + load_halves(message, chans, group)
        beside = beside + ends(message[:chans].astype(F32), base)
    tall = count_y * size_y
    width = 16

    def extended(s, values):
        found = []
        for x in range(size_x):
            part = values[x * tall : (x + 1) * tall]
            found.append(rolled(part, 1 - s * size_y, 0)[:width])
        return jnp.concatenate(found, axis=0)

    tile_out, own_out = outs[0], outs[1]
    tile_out[...] = tile.astype(BF16)
    depth = size_x * width
    own_out[:depth] = extended(0, main)
    own_out[depth:] = extended(0, beside)
    for s in range(1, count_y):
        message = outs[1 + s]
        store_halves(message, 0, extended(s, main))
        edge = extended(s, beside)
        if s not in (1, count_y - 1):
            message[2 * depth :] = with_ends(edge, edge, base).astype(BF16)
            continue
        edge = jnp.concatenate([edge, jnp.zeros((chans - depth, size_z), F32)], axis=0)
        message[2 * depth : 2 * depth + chans] = with_ends(tile, edge, base).astype(BF16)
        at = 2 * depth + chans
        first = size_y - 2 if s == 1 else 0
        for x in range(size_x):
            for y in range(first, first + 2):
                message[at : at + chans] = planes[x, y]
                at += chans


def pack_x_body(count_y, size_x, size_y, chans, tile, own, *refs):
    received = refs[: count_y - 1]
    dens, out = refs[count_y - 1], refs[count_y]
    depth = own.shape[0] // 2
    base = 4 * size_x * size_y
    main, beside = own[:depth], own[depth:]
    for message in received:
        main = main + load_halves(message, 0, depth)
        beside = beside + ends(message[2 * depth : 3 * depth].astype(F32), base)
    dens[:depth] = main
    dens[depth:] = beside
    base = 2 * depth
    below, above = received[0], received[-1]
    size_z = tile.shape[1]
    lane = lanes_of((chans, size_z))
    mine = tile[...].astype(F32)
    low = below[base : base + chans].astype(F32)
    high = above[base : base + chans].astype(F32)
    tall = size_y + 4
    edge = jnp.zeros((chans, size_z), F32)
    for x in range(size_x):
        first = 4 * x * size_y
        to = 4 * x * tall
        edge = jnp.where(
            lane >= to, rolled(low, to - first - 4 * (size_y - 2), 1), edge
        )
        edge = jnp.where(lane >= to + 8, rolled(mine, to + 8 - first, 1), edge)
        edge = jnp.where(
            lane >= to + 8 + 4 * size_y,
            rolled(high, to + 8 + 4 * size_y - first, 1),
            edge,
        )
    beside = jnp.concatenate([beside, jnp.zeros((chans - depth, size_z), F32)], axis=0)
    out[:chans] = with_ends(edge, beside, 4 * size_x * tall).astype(BF16)
    store_halves(out, chans, main)


def spread(tile, y):
    lane = lanes_of(tile.shape)
    size = tile.shape[1]
    turned = rolled(tile, size - 2 - 4 * y, 1)
    keep = (lane < 2) | (lane >= size - 2)
    return jnp.where(keep, turned, 0.0).astype(BF16)


def activate(values):
    return jnp.where(values >= 0, values, 0.2 * values) * jnp.sqrt(jnp.float32(2.0))


def taps_of(stack, weights, taps, y, chans):
    found = None
    for tap, plane in taps:
        rows = stack[plane, pl.ds(y, 3)]
        rows = rows.reshape(3 * chans, rows.shape[-1])
        part = jnp.dot(weights[tap], rows, preferred_element_type=F32)
        found = part if found is None else found + part
    wide = found.shape[1]
    return (
        pltpu.roll(found[:chans], 1, 1)
        + found[chans : 2 * chans]
        + pltpu.roll(found[2 * chans :], wide - 1, 1)
    )


def finish(summed, columns, density):
    copies = summed.shape[1] // columns.shape[2]
    gain = jnp.concatenate([columns[1]] * copies, axis=1)
    bias = jnp.concatenate([columns[0]] * copies, axis=1)
    return activate(summed + gain * density + bias)


def fill(stack, at, main, low, high, start, tile, x, size_y):
    chans, size_z = main.shape[1:]
    tall = size_y + 4
    stack[at, 2 : 2 + size_y, :, :size_z] = main[...]
    for i in range(2):
        rows = slice(start + i * chans, start + (i + 1) * chans)
        stack[at, i, :, :size_z] = low[rows]
        stack[at, tall - 2 + i, :, :size_z] = high[rows]
    edge = tile[:chans].astype(F32)
    for y in range(tall):
        stack[at, y, :, size_z:] = spread(edge, x * tall + y)


def own_body(size_x, size_y, planes, low, high, tile, weights, partial, stack):
    chans = planes.shape[2]
    for x in range(size_x):
        start = low.shape[0] - 2 * (size_x - x) * chans
        fill(stack, x, planes.at[x], low, high, start, tile, x, size_y)
    for at in range(size_x + 2):
        taps = [(e, at + e - 2) for e in range(3) if 0 <= at + e - 2 < size_x]
        for y in range(size_y + 2):
            partial[at, y] = taps_of(stack, weights, taps, y, chans)


def turn_body(below, above, low_side, high_side, first, last):
    chans, _, size_y = below.shape[:3]
    at = 0
    for source, out in ((below, low_side), (above, high_side)):
        for x in range(2):
            part = source[:, x].astype(F32)
            out[x] = jnp.swapaxes(part, 0, 1).astype(BF16)
            for y in range(2):
                first[at : at + chans] = out[x, y]
                last[at : at + chans] = out[x, size_y - 2 + y]
                at += chans


def rest_body(size_x, size_y, *refs):
    partial, main_below, main_above, edge_below, edge_above, low, high = refs[:7]
    dens, first, first_columns, second, second_columns = refs[7:12]
    out, stack, hidden, dense, turned = refs[12:]
    chans, size_z = main_below.shape[2:]
    tall = size_y + 4
    width = 16
    depth = size_x * width
    for i in range(2):
        for side, main, edge, x in (
            (0, main_below, edge_below, size_x - 2 + i),
            (2, main_above, edge_above, i),
        ):
            at = side + i
            fill(stack, at, main.at[i], low, high, 2 * at * chans, edge, x, size_y)
    dense[width : width + depth, :size_z] = dens[:depth]
    dense[width : width + depth, size_z:] = dens[depth:]
    for edge, x, at in (
        (edge_below, size_x - 1, 0),
        (edge_above, 0, width + depth),
    ):
        main = load_halves(edge, chans, depth)
        beside = ends(edge[:depth].astype(F32), 4 * size_x * tall)
        dense[at : at + width, :size_z] = main[x * width : (x + 1) * width]
        dense[at : at + width, size_z:] = beside[x * width : (x + 1) * width]
    for at in range(size_x + 2):
        taps = []
        for e in range(3):
            plane = at + e - 2
            if plane < 0:
                taps.append((e, plane + 2))
            elif plane >= size_x:
                taps.append((e, plane - size_x + 2))
        for y in range(size_y + 2):
            summed = partial[at, y]
            if taps:
                summed = summed + taps_of(stack, first, taps, y, chans)
            density = dense[at * width + y : at * width + y + 1, :]
            hidden[at, y] = finish(summed, first_columns, density).astype(BF16)
    for x in range(size_x):
        for y in range(size_y):
            row = (x + 1) * width + y + 1
            taps = [(e, x + e) for e in range(3)]
            summed = taps_of(hidden, second, taps, y, chans)[:, :size_z]
            density = dense[row : row + 1, :size_z]
            turned[y] = finish(summed, second_columns, density)
        out[:, x] = jnp.swapaxes(turned[...], 0, 1).astype(BF16)


def shards(
    features,
    dest_bricks,
    cell_ids,
    cic_masses,
    live_counts,
    style_vector,
    affine_first,
    kernel_first,
    bias_first,
    gain_first,
    affine_second,
    kernel_second,
    bias_second,
    gain_second,
):
    chans, size_x, size_y, size_z = features.shape
    count_y, count_z = lax.axis_size("gy"), lax.axis_size("gz")
    group = size_x * count_y * size_y
    assert group == chans and 4 * size_x * (size_y + 4) + 4 <= size_z
    depth = size_x * 16
    main_below = shift(features[:, size_x - 2 :], "gx", 1)
    main_above = shift(features[:, :2], "gx", -1)
    painted = call(
        functools.partial(paint_body, count_y, count_z),
        [((size_x, size_y, chans, size_z), BF16)]
        + [((chans + 2 * group, size_z), BF16)] * (count_z - 1)
        + [((2 * group, size_z), F32)],
        fetched=(2, 3, 4, 0),
        late=(0,),
    )(features, live_counts[None, :], dest_bricks.T, cell_ids, cic_masses)
    planes, painted = painted[0], painted[1:]
    from_z = [shift(painted[s - 1], "gz", s) for s in range(1, count_z)]
    rows = [
        2 * depth + ((1 + 2 * size_x) * chans if s in (1, count_y - 1) else depth)
        for s in range(1, count_y)
    ]
    packed = call(
        functools.partial(pack_y_body, count_y, count_z, size_x),
        [((chans, size_z), BF16), ((2 * depth, size_z), F32)]
        + [((r, size_z), BF16) for r in rows],
    )(planes, painted[-1], *from_z)
    from_y = [shift(packed[1 + s], "gy", s) for s in range(1, count_y)]
    modulated = call(
        modulate_body,
        [((3, 3 * chans, 3 * chans), BF16), ((2, chans, size_z), F32)] * 2,
        flops=1 << 22,
        fetched=tuple(range(9)),
    )(
        style_vector[None, :],
        affine_first.T,
        kernel_first,
        bias_first[None, :],
        gain_first[None, :],
        affine_second.T,
        kernel_second,
        bias_second[None, :],
        gain_second[None, :],
    )
    dens, edges = call(
        functools.partial(pack_x_body, count_y, size_x, size_y, chans),
        [
            ((2 * depth, size_z), F32),
            ((chans + 2 * depth, size_z), BF16),
        ],
    )(packed[0], packed[1], *from_y)
    sides = call(
        turn_body,
        [((2, size_y, chans, size_z), BF16)] * 2 + [((8 * chans, size_z), BF16)] * 2,
        flops=1 << 22,
    )(main_below, main_above)
    low = shift(sides[3], "gy", 1)
    high = shift(sides[2], "gy", -1)
    edge_below = shift(edges, "gx", 1)
    edge_above = shift(edges, "gx", -1)
    flops = 2 * 9 * chans * chans * 2 * size_z
    (partial,) = call(
        functools.partial(own_body, size_x, size_y),
        [((size_x + 2, size_y + 2, chans, 2 * size_z), F32)],
        limit=16,
        flops=flops * 3 * size_x * (size_y + 2),
        scratch=[pltpu.VMEM((size_x, size_y + 4, chans, 2 * size_z), BF16)],
    )(planes, from_y[0], from_y[-1], edges, modulated[0])
    (result,) = call(
        functools.partial(rest_body, size_x, size_y),
        [((chans, size_x, size_y, size_z), BF16)],
        limit=24,
        flops=flops * (6 * (size_y + 2) + 3 * size_x * size_y),
        scratch=[
            pltpu.VMEM((4, size_y + 4, chans, 2 * size_z), BF16),
            pltpu.VMEM((size_x + 2, size_y + 2, chans, 2 * size_z), BF16),
            pltpu.VMEM(((size_x + 2) * 16, 2 * size_z), F32),
            pltpu.VMEM((size_y, chans, size_z), F32),
        ],
    )(
        partial,
        *sides[:2],
        edge_below,
        edge_above,
        low,
        high,
        dens,
        *modulated,
    )
    return result


def solution(mesh):
    return jax.shard_map(
        shards,
        mesh=mesh,
        in_specs=(
            P(None, "gx", "gy", "gz"),
            P(("gx", "gy", "gz"), None),
            P(("gx", "gy", "gz"), None),
            P(("gx", "gy", "gz"), None),
            P(("gx", "gy", "gz")),
        )
        + (P(),) * 9,
        out_specs=P(None, "gx", "gy", "gz"),
        check_vma=False,
    )
```

```python
import functools

import jax
import jax.numpy as jnp
from jax import lax
from jax.experimental import pallas as pl
from jax.experimental.pallas import tpu as pltpu
from jax.sharding import PartitionSpec as P


F32 = jnp.float32
BF16 = jnp.bfloat16


def shift(cells, axis, step):
    count = lax.axis_size(axis)
    pairs = [(i, (i + step) % count) for i in range(count)]
    return lax.ppermute(cells, axis, pairs)


def call(body, outs, flops=0, scratch=(), limit=12, fetched=(), late=(), space=pltpu.VMEM):
    def run(*args):
        size = sum(a.size * a.dtype.itemsize for a in args)
        specs = [
            pl.BlockSpec(memory_space=pltpu.HBM if i in fetched else pltpu.VMEM)
            for i in range(len(args))
        ]
        buffers = [pltpu.VMEM(args[i].shape, args[i].dtype) for i in fetched]
        extra = [pltpu.SemaphoreType.DMA((len(fetched),))] if fetched else []

        def wrapped(*refs):
            refs = list(refs)
            if fetched:
                done = refs.pop()
                held = refs[-len(fetched) :]
                refs = refs[: -len(fetched)]
                copies = [
                    pltpu.make_async_copy(refs[i], held[at], done.at[at])
                    for at, i in enumerate(fetched)
                ]
                for copy in copies:
                    copy.start()
                for at, i in enumerate(fetched):
                    refs[i] = held[at]
                    if i not in late:
                        copies[at].wait()
                if late:
                    refs.insert(0, [copies[fetched.index(i)] for i in late])
            body(*refs)

        kernel = pl.pallas_call(
            wrapped,
            out_shape=tuple(jax.ShapeDtypeStruct(s, d) for s, d in outs),
            in_specs=specs,
            out_specs=tuple(pl.BlockSpec(memory_space=space) for _ in outs),
            scratch_shapes=list(scratch) + buffers + extra,
            compiler_params=pltpu.CompilerParams(vmem_limit_bytes=limit << 20),
            cost_estimate=pl.CostEstimate(
                flops=flops, bytes_accessed=size, transcendentals=0
            ),
        )
        args = [
            pltpu.with_memory_space_constraint(a, pltpu.HBM) if i in fetched else a
            for i, a in enumerate(args)
        ]
        return kernel(*args)

    return run


def lanes_of(shape):
    return lax.broadcasted_iota(jnp.int32, shape, len(shape) - 1)


def rolled(values, amount, axis):
    amount = amount % values.shape[axis]
    return values if amount == 0 else pltpu.roll(values, amount, axis)


def ends(values, base):
    lane = lanes_of(values.shape)
    high = rolled(values, -(base + 1), 1)
    low = rolled(values, -(base + 3), 1)
    return jnp.where((lane == 0) | (lane == values.shape[1] - 1), high + low, 0.0)


def with_ends(tile, values, base):
    lane = lanes_of(tile.shape)
    high, low = (part.astype(F32) for part in halves(values))
    tile = jnp.where(
        (lane == base) | (lane == base + 1), rolled(high, base + 1, 1), tile
    )
    return jnp.where(
        (lane == base + 2) | (lane == base + 3), rolled(low, base + 3, 1), tile
    )


def halves(values):
    high = values.astype(BF16)
    return high, (values - high.astype(F32)).astype(BF16)


def store_halves(message, start, values):
    size = values.shape[0]
    message[start : start + size], message[start + size : start + 2 * size] = halves(
        values
    )


def load_halves(message, start, size):
    return message[start : start + size].astype(F32) + message[
        start + size : start + 2 * size
    ].astype(F32)


def column_of(row):
    size = row.shape[1]
    wide = jnp.broadcast_to(row, (size, size))
    same = lax.broadcasted_iota(jnp.int32, (size, size), 0) == lanes_of((size, size))
    return jnp.sum(jnp.where(same, wide, jnp.zeros_like(wide)), axis=1, keepdims=True)


def modulate_body(style, *refs):
    for layer in range(2):
        affine, kernel, bias, gain = refs[4 * layer : 4 * layer + 4]
        weights, columns = refs[8 + 2 * layer : 10 + 2 * layer]
        styles = (
            lax.dot_general(
                style[...],
                affine[...],
                (((1,), (1,)), ((), ())),
                precision=lax.Precision.HIGHEST,
                preferred_element_type=F32,
            )
            + 1.0
        )
        chans = kernel.shape[1]
        total = jnp.zeros((chans, kernel.shape[2]), F32)
        for k in range(27):
            scaled = kernel[k].astype(F32) * styles
            total = total + scaled * scaled
        demod = lax.rsqrt(jnp.sum(total, axis=1, keepdims=True) + 1e-08)
        for e in range(3):
            blocks = [
                (kernel[9 * e + k].astype(F32) * styles * demod).astype(BF16)
                for k in range(9)
            ]
            weights[e] = jnp.concatenate(blocks, axis=1)
        columns[0] = jnp.broadcast_to(column_of(bias[...]), columns.shape[1:])
        columns[1] = jnp.broadcast_to(column_of(gain[...]), columns.shape[1:])


def paint_body(count_y, count_z, pending, features, live, dest, cells, masses, *refs):
    size_x = features.shape[1]
    planes, messages, own, own_tile = refs[0], refs[1:-2], refs[-2], refs[-1]
    size_y, chans, size_z = planes.shape[1:]
    blocks, per = cells.shape
    half = blocks // 2
    rank_y, rank_z = lax.axis_index("gy"), lax.axis_index("gz")
    shape = (blocks, per)
    target = jnp.broadcast_to(column_of(dest[...]), shape)
    to_y = lax.div(target, jnp.full(shape, count_z, jnp.int32))
    to_z = target - to_y * count_z - rank_z
    to_y = to_y - rank_y
    to_y = jnp.where(to_y < 0, to_y + count_y, to_y)
    to_z = jnp.where(to_z < 0, to_z + count_z, to_z)
    cell = cells[...]
    cell_row = lax.div(cell, jnp.full(shape, size_z, jnp.int32))
    at_z = cell - cell_row * size_z
    at_x = lax.div(cell_row, jnp.full(shape, size_y, jnp.int32))
    at_y = cell_row - at_x * size_y
    row = ((to_z * size_x + at_x) * count_y + to_y) * size_y + at_y
    alive = lax.broadcasted_iota(jnp.int32, shape, 0) < jnp.broadcast_to(live[...], shape)
    mass = jnp.where(alive, masses[...].astype(F32), 0.0)

    def paired(values):
        return jnp.concatenate([values[:half], values[half:]], axis=1)

    row, at_z, mass = paired(row), paired(at_z), paired(mass)
    width = 2 * per
    group = size_x * count_y * size_y
    total = count_z * group
    iota_rows = lax.broadcasted_iota(jnp.int32, (total, width), 0)
    iota_z = lax.broadcasted_iota(jnp.int32, (size_z, width), 0)
    left, right = [], []
    for r in range(half):
        left.append(
            jnp.where(iota_rows == row[r : r + 1], mass[r : r + 1], 0.0).astype(BF16)
        )
        right.append(jnp.where(iota_z == at_z[r : r + 1], 1.0, 0.0).astype(BF16))
    painted = lax.dot_general(
        jnp.concatenate(left, axis=1),
        jnp.concatenate(right, axis=1),
        (((1,), (1,)), ((), ())),
        preferred_element_type=F32,
    )
    parts = [painted[s * group : (s + 1) * group] for s in range(count_z)]
    lane = lanes_of((group, size_z))

    def beside(s):
        after = parts[(s + 1) % count_z]
        before = parts[(s - 1) % count_z]
        return jnp.where(lane == 0, after, jnp.where(lane == size_z - 1, before, 0.0))

    own[:group] = parts[0]
    own[group:] = beside(0)
    for copy in pending:
        copy.wait()
    for at in range(size_x):
        part = features[:, at].astype(F32)
        planes[at] = jnp.swapaxes(part, 0, 1).astype(BF16)
    lane = lanes_of((chans, size_z))
    tile = jnp.zeros((chans, size_z), F32)
    for x in range(size_x):
        for y in range(size_y):
            j = x * size_y + y
            turned = rolled(planes[x, y].astype(F32), 6 * j + 2, 1)
            tile = jnp.where((lane >= 6 * j) & (lane < 6 * j + 4), turned, tile)
    own_tile[...] = tile.astype(BF16)
    base = 6 * size_x * size_y
    for s in range(1, count_z):
        message = messages[s - 1]
        message[:chans] = with_ends(tile, beside(s), base).astype(BF16)
        store_halves(message, chans, parts[s])


def pack_y_body(count_y, count_z, size_x, *refs):
    planes, own, own_tile = refs[:3]
    received = refs[3 : 2 + count_z]
    outs = refs[2 + count_z :]
    size_y, chans, size_z = planes.shape[1:]
    group = own.shape[0] // 2
    lane = lanes_of((chans, size_z))
    before = received[0][:chans].astype(F32)
    after = received[-1][:chans].astype(F32)
    mine = own_tile[...].astype(F32)
    place = lane % 6
    tile = jnp.where(place == 3, rolled(mine, 2, 1), rolled(after, 2, 1))
    tile = jnp.where(place == 2, mine, tile)
    tile = jnp.where(place < 2, before, tile)
    base = 6 * size_x * size_y
    main, beside = own[:group], own[group:]
    for message in received:
        main = main + load_halves(message, chans, group)
        beside = beside + ends(message[:chans].astype(F32), base)
    tall = count_y * size_y
    width = 16

    def extended(s, values):
        found = []
        for x in range(size_x):
            part = values[x * tall : (x + 1) * tall]
            found.append(rolled(part, 1 - s * size_y, 0)[:width])
        return jnp.concatenate(found, axis=0)

    tile_out, own_out = outs[0], outs[1]
    tile_out[...] = tile.astype(BF16)
    depth = size_x * width
    own_out[:depth] = extended(0, main)
    own_out[depth:] = extended(0, beside)
    for s in range(1, count_y):
        message = outs[1 + s]
        store_halves(message, 0, extended(s, main))
        edge = extended(s, beside)
        if s not in (1, count_y - 1):
            message[2 * depth :] = with_ends(edge, edge, base).astype(BF16)
            continue
        edge = jnp.concatenate([edge, jnp.zeros((chans - depth, size_z), F32)], axis=0)
        message[2 * depth : 2 * depth + chans] = with_ends(tile, edge, base).astype(BF16)
        at = 2 * depth + chans
        first = size_y - 2 if s == 1 else 0
        for x in range(size_x):
            for y in range(first, first + 2):
                message[at : at + chans] = planes[x, y]
                at += chans


def pack_x_body(count_y, size_x, size_y, chans, tile, own, *refs):
    received = refs[: count_y - 1]
    dens, out = refs[count_y - 1], refs[count_y]
    depth = own.shape[0] // 2
    base = 6 * size_x * size_y
    main, beside = own[:depth], own[depth:]
    for message in received:
        main = main + load_halves(message, 0, depth)
        beside = beside + ends(message[2 * depth : 3 * depth].astype(F32), base)
    dens[:depth] = main
    dens[depth:] = beside
    base = 2 * depth
    below, above = received[0], received[-1]
    size_z = tile.shape[1]
    lane = lanes_of((chans, size_z))
    mine = tile[...].astype(F32)
    low = below[base : base + chans].astype(F32)
    high = above[base : base + chans].astype(F32)
    tall = size_y + 4
    beside = jnp.concatenate([beside, jnp.zeros((chans - depth, size_z), F32)], axis=0)
    for x in range(size_x):
        first = 6 * x * size_y
        edge = rolled(low, -first - 6 * (size_y - 2), 1)
        edge = jnp.where(lane >= 12, rolled(mine, 12 - first, 1), edge)
        at = 12 + 6 * size_y
        edge = jnp.where(lane >= at, rolled(high, at - first, 1), edge)
        if x == 0:
            edge = with_ends(edge, beside, 6 * tall)
        out[x * chans : (x + 1) * chans] = edge.astype(BF16)
    store_halves(out, size_x * chans, main)


def activate(values):
    return jnp.where(values >= 0, values, 0.2 * values) * jnp.sqrt(jnp.float32(2.0))


def finish(summed, columns, density):
    return activate(summed + columns[1] * density + columns[0])


def product(weights, taps, stack, plane, rows):
    chans = weights.shape[1]
    flat = [stack[plane, y : y + 3].reshape(9 * chans, -1) for y in rows]
    matrix = weights[taps].reshape(-1, 9 * chans)
    found = jnp.dot(
        matrix, jnp.concatenate(flat, axis=1), preferred_element_type=F32
    )
    size = flat[0].shape[1]
    return [
        [
            found[e * chans : (e + 1) * chans, i * size : (i + 1) * size]
            for e in range(found.shape[0] // chans)
        ]
        for i in range(len(rows))
    ]


def edge_product(weights, taps, tile, ends_too=False):
    chans = weights.shape[1]
    flat = [rolled(tile, 1 - g - 6 * f, 1) for f in range(3) for g in range(3)]
    taken = jnp.concatenate(flat, axis=0)
    if ends_too:
        lane = lanes_of(tile.shape)
        nothing = jnp.zeros(tile.shape, tile.dtype)
        kept = []
        for f in range(3):
            turned = flat[3 * f + 1]
            kept += [
                jnp.where(lane % 6 == 1, turned, nothing),
                nothing,
                jnp.where(lane % 6 == 4, turned, nothing),
            ]
        taken = jnp.concatenate([taken, jnp.concatenate(kept, axis=0)], axis=1)
    matrix = weights[taps].reshape(-1, 9 * chans)
    found = jnp.dot(matrix, taken, preferred_element_type=F32)
    return [found[e * chans : (e + 1) * chans] for e in range(found.shape[0] // chans)]


def swapped(tile):
    lane = lanes_of(tile.shape)
    return jnp.where(lane % 6 == 1, rolled(tile, -3, 1), rolled(tile, 1, 1))


def put(stack, plane, row, cells, inward):
    lane = lanes_of(cells.shape)
    last = cells.shape[1] - 1
    ends_of = rolled(inward, -6 * row - 2, 1)
    stack[plane, row, 0] = jnp.where(lane == 0, ends_of, rolled(cells, 1, 1))
    stack[plane, row, 1] = cells
    stack[plane, row, 2] = jnp.where(lane == last, ends_of, rolled(cells, -1, 1))


def fill(stack, at, main, low, high, start, tile, size_y):
    chans = main.shape[1]
    inward = swapped(tile)
    for y in range(size_y):
        put(stack, at, 2 + y, main[y], inward)
    for i in range(2):
        rows = slice(start + i * chans, start + (i + 1) * chans)
        put(stack, at, i, low[rows], inward)
        put(stack, at, size_y + 2 + i, high[rows], inward)


def pairs_of(rows):
    return [range(y, min(y + 2, rows)) for y in range(0, rows, 2)]


def sides_of(size_x, below, above):
    return (
        (0, below, ((0, slice(0, 1), (0,)), (1, slice(0, 2), (1, 0)))),
        (
            2,
            above,
            (
                (0, slice(1, 3), (size_x + 1, size_x)),
                (1, slice(2, 3), (size_x + 1,)),
            ),
        ),
    )


def own_body(size_x, size_y, *refs):
    planes, low, high, tiles, below, above, weights = refs[:7]
    partial, partial_edge, stack, beside = refs[7:]
    chans, size_z = planes.shape[2:]
    whole = slice(0, 3)
    for x in range(size_x):
        start = low.shape[0] - 2 * (size_x - x) * chans
        tile = tiles[x * chans : (x + 1) * chans]
        fill(stack, x, planes.at[x], low, high, start, tile, size_y)

        def add(out, at, values, fresh):
            out[at] = values if fresh else out[at] + values

        for e, values in enumerate(edge_product(weights, whole, tile)):
            at = x + 2 - e
            add(partial_edge, at, values, x == 0 or e == 0)
        for rows in pairs_of(size_y + 2):
            found = product(weights, whole, stack, x, rows)
            for y, parts in zip(rows, found):
                for e, values in enumerate(parts):
                    at = x + 2 - e
                    add(partial, (at, y), values, x == 0 or e == 0)
    nothing = jnp.zeros((chans, size_z), BF16)
    for side, main, plan in sides_of(size_x, below, above):
        for plane, taps, targets in plan:
            at = side + plane
            for y in (0, 1, size_y + 2, size_y + 3):
                beside[at, y] = jnp.zeros((3, chans, size_z), BF16)
            for y in range(size_y):
                put(beside, at, 2 + y, main[plane, y], nothing)
            for rows in pairs_of(size_y + 2):
                found = product(weights, taps, beside, at, rows)
                for y, parts in zip(rows, found):
                    for target, values in zip(targets, parts):
                        partial[target, y] = partial[target, y] + values


def turn_body(below, above, low_side, high_side, first, last):
    chans, _, size_y = below.shape[:3]
    at = 0
    for source, out in ((below, low_side), (above, high_side)):
        for x in range(2):
            part = source[:, x].astype(F32)
            out[x] = jnp.swapaxes(part, 0, 1).astype(BF16)
            for y in range(2):
                first[at : at + chans] = out[x, y]
                last[at : at + chans] = out[x, size_y - 2 + y]
                at += chans


def rest_body(size_x, size_y, *refs):
    partial, partial_edge, edge_below, edge_above, low, high = refs[:6]
    dens, first, first_columns, second, second_columns = refs[6:11]
    out, stack, hidden, total, ready, done = refs[11:]
    chans, size_z = partial.shape[2:]
    tall = size_y + 4
    width = 16
    depth = size_x * width
    own = dens[...]
    density = []
    for x in range(size_x):
        rows = slice(x * width, (x + 1) * width)
        density.append((own[:depth][rows], own[depth:][rows]))
    for edge, x, at in ((edge_below, size_x - 1, 0), (edge_above, 0, size_x + 1)):
        rows = slice(x * width, (x + 1) * width)
        main = load_halves(edge, size_x * chans, depth)
        beside = ends(edge[:depth].astype(F32), 6 * tall)
        density.insert(at, (main[rows], beside[rows]))
    lane = lanes_of((1, size_z))
    edges_at = {at: partial_edge[at] for at in range(size_x + 2)}
    fixes = {}
    rows_at = {}
    nothing = jnp.zeros((3, chans, size_z), BF16)
    idle = jnp.zeros((chans, size_z), BF16)
    for side, edge, plan in sides_of(size_x, edge_below, edge_above):
        for plane, taps, targets in plan:
            at = side + plane
            x = size_x - 2 + plane if side == 0 else plane
            tile = edge[x * chans : (x + 1) * chans]
            found = edge_product(first, taps, tile, ends_too=True)
            for target, values in zip(targets, found):
                edges_at[target] = edges_at[target] + values[:, :size_z]
                fix = values[:, size_z:]
                fixes[target] = fixes[target] + fix if target in fixes else fix
            for i in range(2):
                start = (2 * at + i) * chans
                put(stack, at, i, low[start : start + chans], idle)
                stack[at, 2 + i] = nothing
                put(stack, at, 4 + i, high[start : start + chans], idle)
            for begin, rows in ((0, range(2)), (size_y, range(2, 4))):
                found = product(first, taps, stack, at, rows)
                for i, parts in enumerate(found):
                    for target, values in zip(targets, parts):
                        key = (target, begin + i)
                        rows_at[key] = rows_at[key] + values if key in rows_at else values
    wide = lanes_of((chans, size_z))
    outside = (wide == 0) | (wide == size_z - 1)
    for at in sorted(fixes):
        beside = density[at][1]
        ends_at = jnp.zeros((1, size_z), F32)
        for y in range(size_y + 2):
            row = beside[y : y + 1]
            ends_at = jnp.where(lane == 6 * y + 1, rolled(row, 6 * y + 2, 1), ends_at)
            ends_at = jnp.where(lane == 6 * y + 4, rolled(row, 6 * y + 4, 1), ends_at)
        inward = swapped(finish(edges_at[at], first_columns, ends_at).astype(BF16))
        fix = swapped(fixes[at])
        for y in range(size_y + 2):
            value = partial[at, y]
            value = value + jnp.where(outside, rolled(fix, -6 * y - 2, 1), 0.0)
            if (at, y) in rows_at:
                value = value + rows_at[at, y]
            cells = finish(value, first_columns, density[at][0][y : y + 1])
            put(hidden, at, y, cells.astype(BF16), inward)
    for x in range(1, size_x - 1):
        beside = density[x + 1][1]
        ends_at = jnp.zeros((1, size_z), F32)
        for y in range(size_y + 2):
            row = beside[y : y + 1]
            ends_at = jnp.where(lane == 6 * y + 1, rolled(row, 6 * y + 2, 1), ends_at)
            ends_at = jnp.where(lane == 6 * y + 4, rolled(row, 6 * y + 4, 1), ends_at)
        edge = finish(partial_edge[x + 1], first_columns, ends_at).astype(BF16)
        for y in range(size_y + 2):
            cells = finish(
                partial[x + 1, y], first_columns, density[x + 1][0][y : y + 1]
            )
            put(hidden, x + 1, y, cells.astype(BF16), swapped(edge))
    copies = []
    for plane in range(size_x + 2):
        least = max(0, plane - size_x + 1)
        most = min(2, plane)
        for rows in pairs_of(size_y):
            found = product(second, slice(least, most + 1), hidden, plane, rows)
            for y, parts in zip(rows, found):
                for e, values in enumerate(parts, least):
                    x = plane - e
                    if e > 0:
                        values = total[x, y] + values
                    if e == 2:
                        values = finish(
                            values, second_columns, density[x + 1][0][y + 1 : y + 2]
                        )
                    total[x, y] = values
        x = plane - 2
        if x >= 0:
            ready[x] = jnp.swapaxes(total[x], 0, 1).astype(BF16)
            copies.append(pltpu.make_async_copy(ready.at[x], out.at[:, x], done.at[x]))
            copies[-1].start()
    for copy in copies:
        copy.wait()


def shards(
    features,
    dest_bricks,
    cell_ids,
    cic_masses,
    live_counts,
    style_vector,
    affine_first,
    kernel_first,
    bias_first,
    gain_first,
    affine_second,
    kernel_second,
    bias_second,
    gain_second,
):
    chans, size_x, size_y, size_z = features.shape
    count_y, count_z = lax.axis_size("gy"), lax.axis_size("gz")
    group = size_x * count_y * size_y
    assert group == chans and size_x >= 2 and 6 * size_x * size_y + 4 <= size_z
    depth = size_x * 16
    main_below = shift(features[:, size_x - 2 :], "gx", 1)
    main_above = shift(features[:, :2], "gx", -1)
    painted = call(
        functools.partial(paint_body, count_y, count_z),
        [((size_x, size_y, chans, size_z), BF16)]
        + [((chans + 2 * group, size_z), BF16)] * (count_z - 1)
        + [((2 * group, size_z), F32), ((chans, size_z), BF16)],
        fetched=(2, 3, 4, 0),
        late=(0,),
    )(features, live_counts[None, :], dest_bricks.T, cell_ids, cic_masses)
    planes, painted = painted[0], painted[1:]
    from_z = [shift(painted[s - 1], "gz", s) for s in range(1, count_z)]
    rows = [
        2 * depth + ((1 + 2 * size_x) * chans if s in (1, count_y - 1) else depth)
        for s in range(1, count_y)
    ]
    packed = call(
        functools.partial(pack_y_body, count_y, count_z, size_x),
        [((chans, size_z), BF16), ((2 * depth, size_z), F32)]
        + [((r, size_z), BF16) for r in rows],
    )(planes, *painted[-2:], *from_z)
    from_y = [shift(packed[1 + s], "gy", s) for s in range(1, count_y)]
    modulated = call(
        modulate_body,
        [((3, chans, 9 * chans), BF16), ((2, chans, size_z), F32)] * 2,
        flops=1 << 22,
        fetched=tuple(range(9)),
    )(
        style_vector[None, :],
        affine_first.T,
        kernel_first,
        bias_first[None, :],
        gain_first[None, :],
        affine_second.T,
        kernel_second,
        bias_second[None, :],
        gain_second[None, :],
    )
    dens, edges = call(
        functools.partial(pack_x_body, count_y, size_x, size_y, chans),
        [
            ((2 * depth, size_z), F32),
            ((size_x * chans + 2 * depth, size_z), BF16),
        ],
    )(packed[0], packed[1], *from_y)
    sides = call(
        turn_body,
        [((2, size_y, chans, size_z), BF16)] * 2 + [((8 * chans, size_z), BF16)] * 2,
        flops=1 << 22,
    )(main_below, main_above)
    low = shift(sides[3], "gy", 1)
    high = shift(sides[2], "gy", -1)
    edge_below = shift(edges, "gx", 1)
    edge_above = shift(edges, "gx", -1)
    flops = 2 * 9 * chans * chans * size_z
    partial = call(
        functools.partial(own_body, size_x, size_y),
        [
            ((size_x + 2, size_y + 2, chans, size_z), F32),
            ((size_x + 2, chans, size_z), F32),
        ],
        limit=16,
        flops=flops * 3 * size_x * (size_y + 2),
        scratch=[
            pltpu.VMEM((size_x, size_y + 4, 3, chans, size_z), BF16),
            pltpu.VMEM((4, size_y + 4, 3, chans, size_z), BF16),
        ],
    )(planes, from_y[0], from_y[-1], edges, *sides[:2], modulated[0])
    (result,) = call(
        functools.partial(rest_body, size_x, size_y),
        [((chans, size_x, size_y, size_z), BF16)],
        limit=24,
        space=pltpu.HBM,
        flops=flops * (6 * (size_y + 2) + 3 * size_x * size_y),
        scratch=[
            pltpu.VMEM((4, 6, 3, chans, size_z), BF16),
            pltpu.VMEM((size_x + 2, size_y + 2, 3, chans, size_z), BF16),
            pltpu.VMEM((size_x, size_y, chans, size_z), F32),
            pltpu.VMEM((size_x, chans, size_y, size_z), BF16),
            pltpu.SemaphoreType.DMA((size_x,)),
        ],
    )(
        *partial,
        edge_below,
        edge_above,
        low,
        high,
        dens,
        *modulated,
    )
    return result


def solution(mesh):
    return jax.shard_map(
        shards,
        mesh=mesh,
        in_specs=(
            P(None, "gx", "gy", "gz"),
            P(("gx", "gy", "gz"), None),
            P(("gx", "gy", "gz"), None),
            P(("gx", "gy", "gz"), None),
            P(("gx", "gy", "gz")),
        )
        + (P(),) * 9,
        out_specs=P(None, "gx", "gy", "gz"),
        check_vma=False,
    )
```

```python
import functools

import jax
import jax.numpy as jnp
from jax import lax
from jax.experimental import pallas as pl
from jax.experimental.pallas import tpu as pltpu
from jax.sharding import PartitionSpec as P


F32 = jnp.float32
BF16 = jnp.bfloat16


def shift(cells, axis, step):
    count = lax.axis_size(axis)
    pairs = [(i, (i + step) % count) for i in range(count)]
    return lax.ppermute(cells, axis, pairs)


def call(body, outs, flops=0, scratch=(), limit=12, fetched=(), late=(), space=pltpu.VMEM):
    def run(*args):
        size = sum(a.size * a.dtype.itemsize for a in args)
        specs = [
            pl.BlockSpec(memory_space=pltpu.HBM if i in fetched else pltpu.VMEM)
            for i in range(len(args))
        ]
        buffers = [pltpu.VMEM(args[i].shape, args[i].dtype) for i in fetched]
        extra = [pltpu.SemaphoreType.DMA((len(fetched),))] if fetched else []

        def wrapped(*refs):
            refs = list(refs)
            if fetched:
                done = refs.pop()
                held = refs[-len(fetched) :]
                refs = refs[: -len(fetched)]
                copies = [
                    pltpu.make_async_copy(refs[i], held[at], done.at[at])
                    for at, i in enumerate(fetched)
                ]
                for copy in copies:
                    copy.start()
                for at, i in enumerate(fetched):
                    refs[i] = held[at]
                    if i not in late:
                        copies[at].wait()
                if late:
                    refs.insert(0, [copies[fetched.index(i)] for i in late])
            body(*refs)

        kernel = pl.pallas_call(
            wrapped,
            out_shape=tuple(jax.ShapeDtypeStruct(s, d) for s, d in outs),
            in_specs=specs,
            out_specs=tuple(pl.BlockSpec(memory_space=space) for _ in outs),
            scratch_shapes=list(scratch) + buffers + extra,
            compiler_params=pltpu.CompilerParams(vmem_limit_bytes=limit << 20),
            cost_estimate=pl.CostEstimate(
                flops=flops, bytes_accessed=size, transcendentals=0
            ),
        )
        args = [
            pltpu.with_memory_space_constraint(a, pltpu.HBM) if i in fetched else a
            for i, a in enumerate(args)
        ]
        return kernel(*args)

    return run


def lanes_of(shape):
    return lax.broadcasted_iota(jnp.int32, shape, len(shape) - 1)


def rolled(values, amount, axis):
    amount = amount % values.shape[axis]
    return values if amount == 0 else pltpu.roll(values, amount, axis)


def ends(values, base):
    lane = lanes_of(values.shape)
    high = rolled(values, -(base + 1), 1)
    low = rolled(values, -(base + 3), 1)
    return jnp.where((lane == 0) | (lane == values.shape[1] - 1), high + low, 0.0)


def with_ends(tile, values, base):
    lane = lanes_of(tile.shape)
    high, low = (part.astype(F32) for part in halves(values))
    tile = jnp.where(
        (lane == base) | (lane == base + 1), rolled(high, base + 1, 1), tile
    )
    return jnp.where(
        (lane == base + 2) | (lane == base + 3), rolled(low, base + 3, 1), tile
    )


def halves(values):
    high = values.astype(BF16)
    return high, (values - high.astype(F32)).astype(BF16)


def store_halves(message, start, values):
    size = values.shape[0]
    message[start : start + size], message[start + size : start + 2 * size] = halves(
        values
    )


def load_halves(message, start, size):
    return message[start : start + size].astype(F32) + message[
        start + size : start + 2 * size
    ].astype(F32)


def column_of(row):
    size = row.shape[1]
    wide = jnp.broadcast_to(row, (size, size))
    same = lax.broadcasted_iota(jnp.int32, (size, size), 0) == lanes_of((size, size))
    return jnp.sum(jnp.where(same, wide, jnp.zeros_like(wide)), axis=1, keepdims=True)


def modulate_body(style, *refs):
    for layer in range(2):
        affine, kernel, bias, gain = refs[4 * layer : 4 * layer + 4]
        weights, columns = refs[8 + 2 * layer : 10 + 2 * layer]
        styles = (
            lax.dot_general(
                style[...],
                affine[...],
                (((1,), (1,)), ((), ())),
                precision=lax.Precision.HIGHEST,
                preferred_element_type=F32,
            )
            + 1.0
        )
        chans = kernel.shape[1]
        total = jnp.zeros((chans, kernel.shape[2]), F32)
        for k in range(27):
            scaled = kernel[k].astype(F32) * styles
            total = total + scaled * scaled
        demod = lax.rsqrt(jnp.sum(total, axis=1, keepdims=True) + 1e-08)
        for e in range(3):
            blocks = [
                (kernel[9 * e + k].astype(F32) * styles * demod).astype(BF16)
                for k in range(9)
            ]
            weights[e] = jnp.concatenate(blocks, axis=1)
        columns[0] = jnp.broadcast_to(column_of(bias[...]), columns.shape[1:])
        columns[1] = jnp.broadcast_to(column_of(gain[...]), columns.shape[1:])


def paint_body(count_y, count_z, pending, features, live, dest, cells, masses, *refs):
    size_x = features.shape[1]
    planes, messages, own, own_tile = refs[0], refs[1:-2], refs[-2], refs[-1]
    size_y, chans, size_z = planes.shape[1:]
    blocks, per = cells.shape
    half = blocks // 2
    rank_y, rank_z = lax.axis_index("gy"), lax.axis_index("gz")
    shape = (blocks, per)
    target = jnp.broadcast_to(column_of(dest[...]), shape)
    to_y = lax.div(target, jnp.full(shape, count_z, jnp.int32))
    to_z = target - to_y * count_z - rank_z
    to_y = to_y - rank_y
    to_y = jnp.where(to_y < 0, to_y + count_y, to_y)
    to_z = jnp.where(to_z < 0, to_z + count_z, to_z)
    cell = cells[...]
    cell_row = lax.div(cell, jnp.full(shape, size_z, jnp.int32))
    at_z = cell - cell_row * size_z
    at_x = lax.div(cell_row, jnp.full(shape, size_y, jnp.int32))
    at_y = cell_row - at_x * size_y
    row = ((to_z * size_x + at_x) * count_y + to_y) * size_y + at_y
    alive = lax.broadcasted_iota(jnp.int32, shape, 0) < jnp.broadcast_to(live[...], shape)
    mass = jnp.where(alive, masses[...].astype(F32), 0.0)

    def paired(values):
        return jnp.concatenate([values[:half], values[half:]], axis=1)

    row, at_z, mass = paired(row), paired(at_z), paired(mass)
    width = 2 * per
    group = size_x * count_y * size_y
    total = count_z * group
    iota_rows = lax.broadcasted_iota(jnp.int32, (total, width), 0)
    iota_z = lax.broadcasted_iota(jnp.int32, (size_z, width), 0)
    left, right = [], []
    for r in range(half):
        left.append(
            jnp.where(iota_rows == row[r : r + 1], mass[r : r + 1], 0.0).astype(BF16)
        )
        right.append(jnp.where(iota_z == at_z[r : r + 1], 1.0, 0.0).astype(BF16))
    painted = lax.dot_general(
        jnp.concatenate(left, axis=1),
        jnp.concatenate(right, axis=1),
        (((1,), (1,)), ((), ())),
        preferred_element_type=F32,
    )
    parts = [painted[s * group : (s + 1) * group] for s in range(count_z)]
    lane = lanes_of((group, size_z))

    def beside(s):
        after = parts[(s + 1) % count_z]
        before = parts[(s - 1) % count_z]
        return jnp.where(lane == 0, after, jnp.where(lane == size_z - 1, before, 0.0))

    own[:group] = parts[0]
    own[group:] = beside(0)
    for copy in pending:
        copy.wait()
    for at in range(size_x):
        part = features[:, at].astype(F32)
        planes[at] = jnp.swapaxes(part, 0, 1).astype(BF16)
    lane = lanes_of((chans, size_z))
    tile = jnp.zeros((chans, size_z), F32)
    for x in range(size_x):
        for y in range(size_y):
            j = x * size_y + y
            turned = rolled(planes[x, y].astype(F32), 6 * j + 2, 1)
            tile = jnp.where((lane >= 6 * j) & (lane < 6 * j + 4), turned, tile)
    own_tile[...] = tile.astype(BF16)
    base = 6 * size_x * size_y
    for s in range(1, count_z):
        message = messages[s - 1]
        message[:chans] = with_ends(tile, beside(s), base).astype(BF16)
        store_halves(message, chans, parts[s])


def pack_y_body(count_y, count_z, size_x, *refs):
    planes, own, own_tile = refs[:3]
    received = refs[3 : 2 + count_z]
    outs = refs[2 + count_z :]
    size_y, chans, size_z = planes.shape[1:]
    group = own.shape[0] // 2
    lane = lanes_of((chans, size_z))
    before = received[0][:chans].astype(F32)
    after = received[-1][:chans].astype(F32)
    mine = own_tile[...].astype(F32)
    place = lane % 6
    tile = jnp.where(place == 3, rolled(mine, 2, 1), rolled(after, 2, 1))
    tile = jnp.where(place == 2, mine, tile)
    tile = jnp.where(place < 2, before, tile)
    base = 6 * size_x * size_y
    main, beside = own[:group], own[group:]
    for message in received:
        main = main + load_halves(message, chans, group)
        beside = beside + ends(message[:chans].astype(F32), base)
    tall = count_y * size_y
    width = 16

    def extended(s, values):
        found = []
        for x in range(size_x):
            part = values[x * tall : (x + 1) * tall]
            found.append(rolled(part, 1 - s * size_y, 0)[:width])
        return jnp.concatenate(found, axis=0)

    tile_out, own_out = outs[0], outs[1]
    tile_out[...] = tile.astype(BF16)
    depth = size_x * width
    own_out[:depth] = extended(0, main)
    own_out[depth:] = extended(0, beside)
    for s in range(1, count_y):
        message = outs[1 + s]
        store_halves(message, 0, extended(s, main))
        edge = extended(s, beside)
        if s not in (1, count_y - 1):
            message[2 * depth :] = with_ends(edge, edge, base).astype(BF16)
            continue
        edge = jnp.concatenate([edge, jnp.zeros((chans - depth, size_z), F32)], axis=0)
        message[2 * depth : 2 * depth + chans] = with_ends(tile, edge, base).astype(BF16)
        at = 2 * depth + chans
        first = size_y - 2 if s == 1 else 0
        for x in range(size_x):
            for y in range(first, first + 2):
                message[at : at + chans] = planes[x, y]
                at += chans


def pack_x_body(count_y, size_x, size_y, chans, tile, own, *refs):
    received = refs[: count_y - 1]
    dens, up, down = refs[count_y - 1 :]
    depth = own.shape[0] // 2
    base = 6 * size_x * size_y
    main, beside = own[:depth], own[depth:]
    for message in received:
        main = main + load_halves(message, 0, depth)
        beside = beside + ends(message[2 * depth : 3 * depth].astype(F32), base)
    dens[:depth] = main
    dens[depth:] = beside
    base = 2 * depth
    below, above = received[0], received[-1]
    size_z = tile.shape[1]
    lane = lanes_of((chans, size_z))
    mine = tile[...].astype(F32)
    low = below[base : base + chans].astype(F32)
    high = above[base : base + chans].astype(F32)
    tall = size_y + 4
    beside = jnp.concatenate([beside, jnp.zeros((chans - depth, size_z), F32)], axis=0)
    for x in range(size_x):
        first = 6 * x * size_y
        edge = rolled(low, -first - 6 * (size_y - 2), 1)
        edge = jnp.where(lane >= 12, rolled(mine, 12 - first, 1), edge)
        at = 12 + 6 * size_y
        edge = jnp.where(lane >= at, rolled(high, at - first, 1), edge)
        if x == 0:
            edge = with_ends(edge, beside, 6 * tall)
        for out in (up, down):
            out[x * chans : (x + 1) * chans] = edge.astype(BF16)
    width = depth // size_x
    store_halves(up, size_x * chans, main[depth - width :])
    store_halves(down, size_x * chans, main[:width])


def activate(values):
    return jnp.where(values >= 0, values, 0.2 * values) * jnp.sqrt(jnp.float32(2.0))


def finish(summed, columns, density):
    return activate(summed + columns[1] * density + columns[0])


def product(weights, taps, stack, plane, rows):
    chans = weights.shape[1]
    flat = [stack[plane, y : y + 3].reshape(9 * chans, -1) for y in rows]
    matrix = weights[taps].reshape(-1, 9 * chans)
    found = jnp.dot(
        matrix, jnp.concatenate(flat, axis=1), preferred_element_type=F32
    )
    size = flat[0].shape[1]
    return [
        [
            found[e * chans : (e + 1) * chans, i * size : (i + 1) * size]
            for e in range(found.shape[0] // chans)
        ]
        for i in range(len(rows))
    ]


def edge_product(weights, taps, tile, ends_too=False):
    chans = weights.shape[1]
    flat = [rolled(tile, 1 - g - 6 * f, 1) for f in range(3) for g in range(3)]
    taken = jnp.concatenate(flat, axis=0)
    if ends_too:
        lane = lanes_of(tile.shape)
        nothing = jnp.zeros(tile.shape, tile.dtype)
        kept = []
        for f in range(3):
            turned = flat[3 * f + 1]
            kept += [
                jnp.where(lane % 6 == 1, turned, nothing),
                nothing,
                jnp.where(lane % 6 == 4, turned, nothing),
            ]
        taken = jnp.concatenate([taken, jnp.concatenate(kept, axis=0)], axis=1)
    matrix = weights[taps].reshape(-1, 9 * chans)
    found = jnp.dot(matrix, taken, preferred_element_type=F32)
    return [found[e * chans : (e + 1) * chans] for e in range(found.shape[0] // chans)]


def swapped(tile):
    lane = lanes_of(tile.shape)
    return jnp.where(lane % 6 == 1, rolled(tile, -3, 1), rolled(tile, 1, 1))


def put(stack, plane, row, cells, inward):
    lane = lanes_of(cells.shape)
    last = cells.shape[1] - 1
    if inward is None:
        ends_of = jnp.zeros(cells.shape, cells.dtype)
    else:
        ends_of = rolled(inward, -6 * row - 2, 1)
    stack[plane, row, 0] = jnp.where(lane == 0, ends_of, rolled(cells, 1, 1))
    stack[plane, row, 1] = cells
    stack[plane, row, 2] = jnp.where(lane == last, ends_of, rolled(cells, -1, 1))


def ends_row(beside):
    lane = lanes_of(beside.shape)
    at = 6 * lax.broadcasted_iota(jnp.int32, beside.shape, 0)
    before = pltpu.roll(beside, 2, 1, stride=6, stride_axis=0)
    after = pltpu.roll(beside, 4, 1, stride=6, stride_axis=0)
    kept = jnp.where(
        lane == at + 1, before, jnp.where(lane == at + 4, after, jnp.zeros_like(beside))
    )
    return jnp.sum(kept, axis=0, keepdims=True)


def fill(stack, at, main, low, high, start, tile, size_y):
    chans = main.shape[1]
    inward = swapped(tile)
    for y in range(size_y):
        put(stack, at, 2 + y, main[y], inward)
    for i in range(2):
        rows = slice(start + i * chans, start + (i + 1) * chans)
        put(stack, at, i, low[rows], inward)
        put(stack, at, size_y + 2 + i, high[rows], inward)


def pairs_of(rows):
    return [range(y, min(y + 2, rows)) for y in range(0, rows, 2)]


def sides_of(size_x, below, above):
    return (
        (0, below, ((0, slice(0, 1), (0,)), (1, slice(0, 2), (1, 0)))),
        (
            2,
            above,
            (
                (0, slice(1, 3), (size_x + 1, size_x)),
                (1, slice(2, 3), (size_x + 1,)),
            ),
        ),
    )


def own_body(size_x, size_y, *refs):
    planes, low, high, tiles, below, above, weights = refs[:7]
    partial, partial_edge, stack, beside = refs[7:]
    chans, size_z = planes.shape[2:]
    whole = slice(0, 3)
    for x in range(size_x):
        start = low.shape[0] - 2 * (size_x - x) * chans
        tile = tiles[x * chans : (x + 1) * chans]
        fill(stack, x, planes.at[x], low, high, start, tile, size_y)

        def add(out, at, values, fresh):
            out[at] = values if fresh else out[at] + values

        for e, values in enumerate(edge_product(weights, whole, tile)):
            at = x + 2 - e
            add(partial_edge, at, values, x == 0 or e == 0)
        for rows in pairs_of(size_y + 2):
            found = product(weights, whole, stack, x, rows)
            for y, parts in zip(rows, found):
                for e, values in enumerate(parts):
                    at = x + 2 - e
                    add(partial, (at, y), values, x == 0 or e == 0)
    for side, main, plan in sides_of(size_x, below, above):
        for plane, taps, targets in plan:
            at = side + plane
            for y in (0, 1, size_y + 2, size_y + 3):
                beside[at, y] = jnp.zeros((3, chans, size_z), BF16)
            for y in range(size_y):
                put(beside, at, 2 + y, main[plane, y], None)
            for rows in pairs_of(size_y + 2):
                found = product(weights, taps, beside, at, rows)
                for y, parts in zip(rows, found):
                    for target, values in zip(targets, parts):
                        partial[target, y] = partial[target, y] + values


def turn_body(below, above, low_side, high_side, first, last):
    chans, _, size_y = below.shape[:3]
    at = 0
    for source, out in ((below, low_side), (above, high_side)):
        for x in range(2):
            part = source[:, x].astype(F32)
            out[x] = jnp.swapaxes(part, 0, 1).astype(BF16)
            for y in range(2):
                first[at : at + chans] = out[x, y]
                last[at : at + chans] = out[x, size_y - 2 + y]
                at += chans


def rest_body(size_x, size_y, *refs):
    partial, partial_edge, edge_below, edge_above, low, high = refs[:6]
    dens, first, first_columns, second, second_columns = refs[6:11]
    out, stack, hidden, total, ready, done = refs[11:]
    chans, size_z = partial.shape[2:]
    tall = size_y + 4
    width = 16
    depth = size_x * width
    own = dens[...]
    density = []
    for x in range(size_x):
        rows = slice(x * width, (x + 1) * width)
        density.append((own[:depth][rows], own[depth:][rows]))
    for edge, x, at in ((edge_below, size_x - 1, 0), (edge_above, 0, size_x + 1)):
        rows = slice(x * width, (x + 1) * width)
        main = load_halves(edge, size_x * chans, width)
        beside = ends(edge[:depth].astype(F32), 6 * tall)
        density.insert(at, (main, beside[rows]))
    edges_at = {at: partial_edge[at] for at in range(size_x + 2)}
    fixes = {}
    rows_at = {}
    nothing = jnp.zeros((3, chans, size_z), BF16)
    for side, edge, plan in sides_of(size_x, edge_below, edge_above):
        for plane, taps, targets in plan:
            at = side + plane
            x = size_x - 2 + plane if side == 0 else plane
            tile = edge[x * chans : (x + 1) * chans]
            found = edge_product(first, taps, tile, ends_too=True)
            for target, values in zip(targets, found):
                edges_at[target] = edges_at[target] + values[:, :size_z]
                fix = values[:, size_z:]
                fixes[target] = fixes[target] + fix if target in fixes else fix
            for i in range(2):
                start = (2 * at + i) * chans
                put(stack, at, i, low[start : start + chans], None)
                stack[at, 2 + i] = nothing
                put(stack, at, 4 + i, high[start : start + chans], None)
            for begin, rows in ((0, range(2)), (size_y, range(2, 4))):
                found = product(first, taps, stack, at, rows)
                for i, parts in enumerate(found):
                    for target, values in zip(targets, parts):
                        key = (target, begin + i)
                        rows_at[key] = rows_at[key] + values if key in rows_at else values
    wide = lanes_of((chans, size_z))
    outside = (wide == 0) | (wide == size_z - 1)
    for at in sorted(fixes):
        beside = density[at][1]
        ends_at = ends_row(beside)
        inward = swapped(finish(edges_at[at], first_columns, ends_at).astype(BF16))
        fix = swapped(fixes[at])
        for y in range(size_y + 2):
            value = partial[at, y]
            value = value + jnp.where(outside, rolled(fix, -6 * y - 2, 1), 0.0)
            if (at, y) in rows_at:
                value = value + rows_at[at, y]
            cells = finish(value, first_columns, density[at][0][y : y + 1])
            put(hidden, at, y, cells.astype(BF16), inward)
    for x in range(1, size_x - 1):
        beside = density[x + 1][1]
        ends_at = ends_row(beside)
        edge = finish(partial_edge[x + 1], first_columns, ends_at).astype(BF16)
        for y in range(size_y + 2):
            cells = finish(
                partial[x + 1, y], first_columns, density[x + 1][0][y : y + 1]
            )
            put(hidden, x + 1, y, cells.astype(BF16), swapped(edge))
    copies = []
    for plane in range(size_x + 2):
        least = max(0, plane - size_x + 1)
        most = min(2, plane)
        for rows in pairs_of(size_y):
            found = product(second, slice(least, most + 1), hidden, plane, rows)
            for y, parts in zip(rows, found):
                for e, values in enumerate(parts, least):
                    x = plane - e
                    if e > 0:
                        values = total[x, y] + values
                    if e == 2:
                        values = finish(
                            values, second_columns, density[x + 1][0][y + 1 : y + 2]
                        )
                    total[x, y] = values
        x = plane - 2
        if x >= 0:
            ready[x] = jnp.swapaxes(total[x], 0, 1).astype(BF16)
            copies.append(pltpu.make_async_copy(ready.at[x], out.at[:, x], done.at[x]))
            copies[-1].start()
    for copy in copies:
        copy.wait()


def shards(
    features,
    dest_bricks,
    cell_ids,
    cic_masses,
    live_counts,
    style_vector,
    affine_first,
    kernel_first,
    bias_first,
    gain_first,
    affine_second,
    kernel_second,
    bias_second,
    gain_second,
):
    chans, size_x, size_y, size_z = features.shape
    count_y, count_z = lax.axis_size("gy"), lax.axis_size("gz")
    group = size_x * count_y * size_y
    assert group == chans and size_x >= 2 and 6 * size_x * size_y + 4 <= size_z
    depth = size_x * 16
    main_below = shift(features[:, size_x - 2 :], "gx", 1)
    main_above = shift(features[:, :2], "gx", -1)
    painted = call(
        functools.partial(paint_body, count_y, count_z),
        [((size_x, size_y, chans, size_z), BF16)]
        + [((chans + 2 * group, size_z), BF16)] * (count_z - 1)
        + [((2 * group, size_z), F32), ((chans, size_z), BF16)],
        fetched=(2, 3, 4, 0),
        late=(0,),
    )(features, live_counts[None, :], dest_bricks.T, cell_ids, cic_masses)
    planes, painted = painted[0], painted[1:]
    from_z = [shift(painted[s - 1], "gz", s) for s in range(1, count_z)]
    rows = [
        2 * depth + ((1 + 2 * size_x) * chans if s in (1, count_y - 1) else depth)
        for s in range(1, count_y)
    ]
    packed = call(
        functools.partial(pack_y_body, count_y, count_z, size_x),
        [((chans, size_z), BF16), ((2 * depth, size_z), F32)]
        + [((r, size_z), BF16) for r in rows],
    )(planes, *painted[-2:], *from_z)
    from_y = [shift(packed[1 + s], "gy", s) for s in range(1, count_y)]
    modulated = call(
        modulate_body,
        [((3, chans, 9 * chans), BF16), ((2, chans, size_z), F32)] * 2,
        flops=1 << 22,
        fetched=tuple(range(9)),
    )(
        style_vector[None, :],
        affine_first.T,
        kernel_first,
        bias_first[None, :],
        gain_first[None, :],
        affine_second.T,
        kernel_second,
        bias_second[None, :],
        gain_second[None, :],
    )
    dens, edges_up, edges = call(
        functools.partial(pack_x_body, count_y, size_x, size_y, chans),
        [
            ((2 * depth, size_z), F32),
            ((size_x * chans + 2 * depth // size_x, size_z), BF16),
            ((size_x * chans + 2 * depth // size_x, size_z), BF16),
        ],
    )(packed[0], packed[1], *from_y)
    sides = call(
        turn_body,
        [((2, size_y, chans, size_z), BF16)] * 2 + [((8 * chans, size_z), BF16)] * 2,
        flops=1 << 22,
    )(main_below, main_above)
    low = shift(sides[3], "gy", 1)
    high = shift(sides[2], "gy", -1)
    edge_below = shift(edges_up, "gx", 1)
    edge_above = shift(edges, "gx", -1)
    flops = 2 * 9 * chans * chans * size_z
    partial = call(
        functools.partial(own_body, size_x, size_y),
        [
            ((size_x + 2, size_y + 2, chans, size_z), F32),
            ((size_x + 2, chans, size_z), F32),
        ],
        limit=16,
        flops=flops * 3 * size_x * (size_y + 2),
        scratch=[
            pltpu.VMEM((size_x, size_y + 4, 3, chans, size_z), BF16),
            pltpu.VMEM((4, size_y + 4, 3, chans, size_z), BF16),
        ],
    )(planes, from_y[0], from_y[-1], edges, *sides[:2], modulated[0])
    (result,) = call(
        functools.partial(rest_body, size_x, size_y),
        [((chans, size_x, size_y, size_z), BF16)],
        limit=24,
        space=pltpu.HBM,
        flops=flops * (6 * (size_y + 2) + 3 * size_x * size_y),
        scratch=[
            pltpu.VMEM((4, 6, 3, chans, size_z), BF16),
            pltpu.VMEM((size_x + 2, size_y + 2, 3, chans, size_z), BF16),
            pltpu.VMEM((size_x, size_y, chans, size_z), F32),
            pltpu.VMEM((size_x, chans, size_y, size_z), BF16),
            pltpu.SemaphoreType.DMA((size_x,)),
        ],
    )(
        *partial,
        edge_below,
        edge_above,
        low,
        high,
        dens,
        *modulated,
    )
    return result


def solution(mesh):
    return jax.shard_map(
        shards,
        mesh=mesh,
        in_specs=(
            P(None, "gx", "gy", "gz"),
            P(("gx", "gy", "gz"), None),
            P(("gx", "gy", "gz"), None),
            P(("gx", "gy", "gz"), None),
            P(("gx", "gy", "gz")),
        )
        + (P(),) * 9,
        out_specs=P(None, "gx", "gy", "gz"),
        check_vma=False,
    )
```
